768 devices in a mesh: dp: 96 (over x, z, core), chan: 8 (over y).
Axes of the slice: x: 4, y: 8, z: 12, core: 2. Of those that a mesh axis runs over, the one named last changes fastest.
Arguments:
- features: bfloat16 [96, 16, 16, 1024], P('dp'), may hold values from -6 to 6
- styles: float32 [96, 1024], P('dp'), may hold values from 0.3 to 3
- conv_weight: bfloat16 [9, 1024, 1024], P(None, None, 'chan'), may hold values from -0.0625 to 0.0625
- grad_out: bfloat16 [96, 16, 16, 1024], P('dp', None, None, 'chan'), may hold values from -6 to 6
- crossover: int32 [96], P('dp'), may hold values from 0 to 13
- partner: int32 [96], P('dp'), may hold values from 0 to 95
- latents: float32 [96, 1024], P('dp'), may hold values from -6 to 6
- map_pre: float32 [96, 1024], P('dp'), may hold values from -6 to 6
- map_weight: float32 [1024, 1024], P(None, 'chan'), may hold values from -0.1875 to 0.1875
Outputs:
- grad_weight: float32 [9216, 1024], P('dp', 'chan')
- grad_input: bfloat16 [96, 16, 16, 1024], P('dp', None, None, 'chan')
- grad_map_out: float32 [1024, 1024], P(None, 'chan')
- grad_map_in: float32 [1024, 1024], P(None, 'chan')
The draws below stay inside these ranges and needn't reach their ends.
All inputs are finite; a program needn't handle non-finite values.
Results may differ from the reference program's by a relative error of at most 0.005.
Values sent between devices are 32-bit elements; how exact they have to be, the bound alone decides.
No kernel may reach another device: no remote copies, remote signals or barrier semaphores. Data moves between devices by JAX's collectives and lax.ppermute only.
A program may use at most 64 MiB of HBM per device.

```python
import math
import jax
import jax.numpy as jnp
import numpy as np
from jax import lax

C = 1024
HID = 1024
LAT = 1024
KTAPS = 9
RES = 16
LAYER = 6
LAYERS = 14
BATCH = 96


def place_ends(entries, own_key, least, high):
    extent = entries.shape
    spot = [jax.random.randint(jax.random.fold_in(own_key, axis), (), 0, extent[axis]) for axis in range(len(extent))]
    entries = entries.at[tuple(spot)].set(least)
    longest = extent.index(max(extent))
    spot[longest] = (spot[longest] + 1) % extent[longest]
    return entries.at[tuple(spot)].set(high)


def block_scale(rng, extent, split, low, largest):
    loudness, own = 1.0, jax.random.fold_in(rng, 6)
    for axis_at, blocks in split:
        draws = jnp.exp(jax.random.uniform(jax.random.fold_in(own, axis_at), (blocks,), jnp.float32, low / len(split), largest / len(split)))
        loudness = loudness * jnp.repeat(draws, extent[axis_at] // blocks).reshape([-1 if axis == axis_at else 1 for axis in range(len(extent))])
    return loudness


def cumulative_ranks(number_of, lean):
    weights = [(1 << 20) // math.isqrt(standing ** lean) + 1 for standing in range(1, number_of + 1)]
    width = 1 + sum(weights) // (1 << 30)
    return np.cumsum(np.array([max(1, weight // width) for weight in weights]))


def skewed_ids(own_key, dims, count, slope):
    listing = cumulative_ranks(count, slope)
    ticket = jax.random.randint(jax.random.fold_in(own_key, 1), dims, 0, int(listing[count - 1]))
    rank = jnp.searchsorted(jnp.asarray(listing, jnp.int32), ticket, side="right")
    return jax.random.permutation(jax.random.fold_in(own_key, 2), count)[rank].astype(jnp.int32)


def centred(rng, dims, spread, bound, shards=(), kind=jnp.bfloat16):
    values = spread * jax.random.normal(rng, dims, jnp.float32)
    if shards:
        values = values * block_scale(rng, dims, shards, -0.22, 0.18)
    return jnp.clip(values, -bound, bound).astype(kind)


def setup_inputs(seed: int = 0) -> dict:
    seeds = jax.random.split(jax.random.key(seed), 10)
    return {
        "features": centred(seeds[0], (BATCH, RES, RES, C), 1.0, 6.0, ((0, 96),)),
        "styles": jnp.clip(jnp.exp(math.log(3.0) - 2.3025851 * jax.random.uniform(seeds[1], (BATCH, C), jnp.float32) ** block_scale(seeds[1], (BATCH, C), ((0, 96),), -0.2, 0.2)), 0.3, 3.0),
        "conv_weight": centred(seeds[2], (KTAPS, C, C), (KTAPS * C) ** -0.5, 0.0625, ((2, 8),)),
        "grad_out": centred(seeds[3], (BATCH, RES, RES, C), 1.0, 6.0, ((0, 96), (3, 8))),
        "crossover": place_ends(jax.random.randint(seeds[4], (BATCH,), 0, LAYERS), jax.random.fold_in(seeds[4], 1), 0, LAYERS - 1).astype(jnp.int32),
        "partner": place_ends(skewed_ids(seeds[5], (BATCH,), BATCH, 2), jax.random.fold_in(seeds[5], 3), 0, BATCH - 1).astype(jnp.int32),
        "latents": centred(seeds[6], (BATCH, LAT), 1.0, 6.0, ((0, 96),), jnp.float32),
        "map_pre": centred(seeds[7], (BATCH, HID), 1.0, 6.0, ((0, 96),), jnp.float32),
        "map_weight": centred(seeds[8], (HID, C), HID ** -0.5, 0.1875, ((1, 8),), jnp.float32),
    }


highest = lax.Precision.HIGHEST

def tap_window(padded, tap_index, side_len):
    row_off = tap_index // 3
    col_off = tap_index % 3
    return padded[:, row_off:row_off + side_len, col_off:col_off + side_len, :]

def reference(features, styles, conv_weight, grad_out, crossover, partner, latents, map_pre, map_weight):
    batch_size = features.shape[0]
    side_len = features.shape[1]
    channels = features.shape[3]
    pixels = batch_size * side_len * side_len
    scaled = (features.astype(jnp.float32) * styles[:, None, None, :]).astype(jnp.bfloat16)
    weight_wide = conv_weight.astype(jnp.float32)
    weight_sq = lax.optimization_barrier(jnp.sum(weight_wide * weight_wide, axis=0))
    style_sq = styles * styles
    demodulate = lax.rsqrt(jnp.dot(style_sq, weight_sq, precision=highest) + 1e-08)
    padded = jnp.pad(scaled, ((0, 0), (1, 1), (1, 1), (0, 0)))
    conv_out = jnp.zeros((pixels, channels), jnp.float32)
    for tap_index in range(KTAPS):
        window = tap_window(padded, tap_index, side_len).reshape(pixels, channels)
        conv_out = conv_out + jnp.dot(window, conv_weight[tap_index], preferred_element_type=jnp.float32)
    grad_wide = grad_out.astype(jnp.float32).reshape(batch_size, side_len * side_len, channels)
    demod_grad = lax.optimization_barrier(jnp.sum(grad_wide * conv_out.reshape(batch_size, side_len * side_len, channels), axis=1))
    square_grad = -0.5 * demodulate ** 3 * demod_grad
    grad_scaled = (grad_wide * demodulate[:, None, :]).astype(jnp.bfloat16).reshape(pixels, channels)
    accumulated = jnp.zeros((batch_size, side_len + 2, side_len + 2, channels), jnp.float32)
    weight_rows = []
    for tap_index in range(KTAPS):
        row_off = tap_index // 3
        col_off = tap_index % 3
        product_piece = lax.dot_general(grad_scaled, conv_weight[tap_index], (((1,), (1,)), ((), ())), preferred_element_type=jnp.float32)
        accumulated = accumulated.at[:, row_off:row_off + side_len, col_off:col_off + side_len, :].add(product_piece.reshape(batch_size, side_len, side_len, channels))
        window = tap_window(padded, tap_index, side_len).reshape(pixels, channels)
        weight_rows.append(lax.dot_general(window, grad_scaled, (((0,), (0,)), ((), ())), preferred_element_type=jnp.float32))
    grad_inner = accumulated[:, 1:-1, 1:-1, :]
    grad_input = (grad_inner * styles[:, None, None, :]).astype(jnp.bfloat16)
    style_grad = lax.optimization_barrier(jnp.sum(grad_inner * features.astype(jnp.float32), axis=(1, 2))) + 2.0 * styles * jnp.dot(square_grad, weight_sq.T, precision=highest)
    style_factor = jnp.dot(style_sq.T, square_grad, precision=highest)
    grad_weight = (jnp.stack(weight_rows) + 2.0 * weight_wide * style_factor[None]) / batch_size
    grad_weight = grad_weight.reshape(KTAPS * channels, channels)
    sample_ids = jnp.arange(batch_size, dtype=jnp.int32)
    source = jnp.where(crossover <= LAYER, partner, sample_ids).astype(jnp.int32)
    incoming = jax.ops.segment_sum(style_grad, source, num_segments=batch_size)
    hidden = jnp.where(map_pre > 0, map_pre, 0.2 * map_pre)
    grad_map_out = jnp.dot(hidden.T, incoming, precision=highest) / batch_size
    hidden_grad = jnp.dot(incoming, map_weight.T, precision=highest)
    pre_grad = hidden_grad * jnp.where(map_pre > 0, 1.0, 0.2).astype(map_pre.dtype)
    grad_map_in = jnp.dot(latents.T, pre_grad, precision=highest) / batch_size
    return (grad_weight, grad_input, grad_map_out, grad_map_in)
```

```python
import jax
import jax.numpy as jnp
from jax import lax
from jax.sharding import Mesh, PartitionSpec as P

KTAPS = 9
LAYER = 6
LANES = 128

highest = lax.Precision.HIGHEST


def dp_axes(dp_count):
    return (4, 12, 2) if dp_count == 96 else (2, dp_count // 4, 2)


def tap_window(padded, row_off, col_off, side_len):
    return padded[:, row_off : row_off + side_len, col_off : col_off + side_len, :]


def exchange(blocks, axes):
    return lax.all_to_all(blocks, axes, 0, 0, tiled=True)


def local(
    features, styles, conv_weight, grad_out, crossover, partner, latents, map_pre, map_weight
):
    samples, side_len, _, channels = features.shape
    cols_dev = conv_weight.shape[2]
    pixels = samples * side_len * side_len
    nx, nz, ncore, nchan = (lax.axis_size(name) for name in ("x", "z", "core", "chan"))
    batch_size = nx * nz * ncore
    rows_dev = KTAPS * channels // batch_size
    chan_id = lax.axis_index("chan")
    dp_id = (lax.axis_index("x") * nz + lax.axis_index("z")) * ncore + lax.axis_index("core")

    own_rows = jnp.concatenate(
        [latents.reshape(1, -1, LANES), map_pre.reshape(1, -1, LANES)], axis=1
    )
    gathered = exchange(
        jnp.broadcast_to(own_rows, (batch_size,) + own_rows.shape[1:]), ("x", "z", "core")
    )
    map_rows = exchange(map_weight.reshape(nchan, -1, cols_dev), "chan")

    scaled = (features.astype(jnp.float32) * styles[:, None, None, :]).astype(jnp.bfloat16)
    weight_sq = jnp.sum(jnp.square(conv_weight.astype(jnp.float32)), axis=0)
    style_sq = styles * styles
    demodulate = lax.rsqrt(jnp.dot(style_sq, weight_sq, precision=highest) + 1e-08)
    padded = jnp.pad(scaled, ((0, 0), (1, 1), (1, 1), (0, 0)))
    patches = jnp.concatenate(
        [
            tap_window(padded, tap // 3, tap % 3, side_len).reshape(pixels, channels)
            for tap in range(KTAPS)
        ],
        axis=1,
    )
    weight_flat = conv_weight.reshape(KTAPS * channels, cols_dev)
    conv_out = jnp.dot(patches, weight_flat, preferred_element_type=jnp.float32)
    grad_wide = grad_out.astype(jnp.float32).reshape(pixels, cols_dev)
    demod_grad = jnp.sum(grad_wide * conv_out, axis=0, keepdims=True)
    square_grad = -0.5 * demodulate**3 * demod_grad
    grad_scaled = (grad_wide * demodulate).astype(jnp.bfloat16)
    grad_padded = jnp.pad(
        grad_scaled.reshape(samples, side_len, side_len, cols_dev), ((0, 0), (1, 1), (1, 1), (0, 0))
    )
    inner_part = jnp.zeros((pixels, channels), jnp.float32)
    for tap in range(KTAPS):
        inner_part = inner_part + lax.dot_general(
            tap_window(grad_padded, 2 - tap // 3, 2 - tap % 3, side_len).reshape(pixels, cols_dev),
            conv_weight[tap],
            (((1,), (1,)), ((), ())),
            preferred_element_type=jnp.float32,
        )
    style_part = jnp.sum(
        inner_part * features.reshape(pixels, channels).astype(jnp.float32), axis=0
    ) + (2.0 * styles * jnp.dot(square_grad, weight_sq.T, precision=highest)).reshape(channels)

    grad_inner = lax.psum_scatter(inner_part, "chan", scatter_dimension=1, tiled=True)
    style_cols = lax.dynamic_slice_in_dim(styles, chan_id * cols_dev, cols_dev, 1)
    grad_input = (grad_inner * style_cols).astype(jnp.bfloat16)

    tile = style_part.reshape(1, -1, LANES)
    parts = exchange(
        jnp.broadcast_to(tile, (ncore * nchan,) + tile.shape[1:]), ("core", "chan")
    )
    style_grad = jnp.sum(parts.reshape(ncore, nchan, -1, LANES), axis=1)
    hidden_cols = jnp.sum(
        lax.dot_general(
            map_rows,
            style_grad.reshape(ncore, nchan, cols_dev),
            (((2,), (2,)), ((0,), (1,))),
            precision=highest,
        ),
        axis=0,
    ).T
    style_own = lax.dynamic_slice_in_dim(
        style_grad.reshape(ncore, nchan, cols_dev), chan_id, 1, 1
    ).reshape(ncore, cols_dev)
    source = jnp.where(crossover <= LAYER, partner, dp_id).astype(jnp.float32)
    source = lax.all_gather(
        jnp.broadcast_to(source[:, None], (1, cols_dev)), "core", axis=0, tiled=True
    )

    style_factor = jnp.dot(style_sq.T, square_grad, precision=highest)
    product_rows = lax.dot_general(
        patches, grad_scaled, (((0,), (0,)), ((), ())), preferred_element_type=jnp.float32
    ) + 2.0 * weight_flat.astype(jnp.float32) * jnp.tile(style_factor, (KTAPS, 1))
    pieces = product_rows.reshape(nx * nz, ncore, rows_dev, cols_dev).transpose(1, 0, 2, 3)
    pieces = jnp.sum(exchange(pieces, "core"), axis=0)
    pieces = pieces.reshape(nx, nz * rows_dev, cols_dev)
    pad_rows = jnp.zeros((8 - 3 * ncore, cols_dev), jnp.float32)
    riders = jnp.concatenate([style_own, hidden_cols, source, pad_rows], axis=0)
    moved = exchange(
        jnp.concatenate([pieces, jnp.broadcast_to(riders[None], (nx,) + riders.shape)], axis=1), "x"
    )
    pieces = jnp.sum(moved[:, : nz * rows_dev], axis=0).reshape(nz, rows_dev, cols_dev)
    riders = jnp.concatenate(
        [
            moved[:, nz * rows_dev + kind * ncore : nz * rows_dev + (kind + 1) * ncore].reshape(
                nx * ncore, cols_dev
            )
            for kind in range(3)
        ],
        axis=0,
    )
    moved = exchange(
        jnp.concatenate([pieces, jnp.broadcast_to(riders[None], (nz,) + riders.shape)], axis=1), "z"
    )
    grad_weight = jnp.sum(moved[:, :rows_dev], axis=0) / batch_size

    per = nx * ncore
    style_all, hidden_all, source_all = (
        moved[:, rows_dev + kind * per : rows_dev + (kind + 1) * per].reshape(batch_size, cols_dev)
        for kind in range(3)
    )
    matches = (
        source_all[:, :1] == lax.broadcasted_iota(jnp.int32, (1, batch_size), 1).astype(jnp.float32)
    ).astype(jnp.float32)
    received = lax.dot_general(
        matches,
        jnp.concatenate([style_all, hidden_all], axis=1),
        (((0,), (0,)), ((), ())),
        precision=highest,
    )
    incoming, hidden_grad = received[:, :cols_dev], received[:, cols_dev:]
    half = channels // LANES
    all_latents = gathered[:, :half].reshape(batch_size, -1)
    all_pre = gathered[:, half:].reshape(batch_size, -1)
    hidden = jnp.where(all_pre > 0, all_pre, 0.2 * all_pre)
    grad_map_out = (
        lax.dot_general(hidden, incoming, (((0,), (0,)), ((), ())), precision=highest) / batch_size
    )
    pre_cols = lax.dynamic_slice_in_dim(all_pre, chan_id * cols_dev, cols_dev, 1)
    pre_grad = hidden_grad * jnp.where(pre_cols > 0, 1.0, 0.2)
    grad_map_in = (
        lax.dot_general(all_latents, pre_grad, (((0,), (0,)), ((), ())), precision=highest)
        / batch_size
    )
    return (
        grad_weight,
        grad_input.reshape(samples, side_len, side_len, cols_dev),
        grad_map_out,
        grad_map_in,
    )


def solution(mesh):
    dp_count, chan_count = mesh.devices.shape
    split = Mesh(
        mesh.devices.reshape(dp_axes(dp_count) + (chan_count,)), ("x", "z", "core", "chan")
    )
    dp = ("x", "z", "core")
    in_specs = (
        P(dp, None, None, None),
        P(dp, None),
        P(None, None, "chan"),
        P(dp, None, None, "chan"),
        P(dp),
        P(dp),
        P(dp, None),
        P(dp, None),
        P(None, "chan"),
    )
    out_specs = (P(dp, "chan"), P(dp, None, None, "chan"), P(None, "chan"), P(None, "chan"))
    return jax.shard_map(local, mesh=split, in_specs=in_specs, out_specs=out_specs, check_vma=False)
```

```python
import jax
import jax.numpy as jnp
import numpy as np
from jax import lax
from jax.sharding import Mesh, PartitionSpec as P

KTAPS = 9
LAYER = 6
LANES = 128

highest = lax.Precision.HIGHEST


def dp_axes(dp_count):
    return (4, 12, 2) if dp_count == 96 else (2, dp_count // 4, 2)


def tap_window(padded, row_off, col_off, side_len):
    return padded[:, row_off : row_off + side_len, col_off : col_off + side_len, :]


def exchange(blocks, axes):
    return lax.all_to_all(blocks, axes, 0, 0, tiled=True)


def local(
    features, styles, conv_weight, grad_out, crossover, partner, latents, map_pre, map_weight
):
    samples, side_len, _, channels = features.shape
    cols_dev = conv_weight.shape[2]
    pixels = samples * side_len * side_len
    nx, nz, ncore, nchan = (lax.axis_size(name) for name in ("x", "z", "core", "chan"))
    batch_size = nx * nz * ncore
    rows_dev = KTAPS * channels // batch_size
    chan_id = lax.axis_index("chan")
    dp_id = (lax.axis_index("x") * nz + lax.axis_index("z")) * ncore + lax.axis_index("core")

    gathered = jnp.concatenate(
        [latents.reshape(1, -1, LANES), map_pre.reshape(1, -1, LANES)], axis=1
    )
    offsets = np.zeros((3, 1), np.int32)
    for name, axis in (("z", 1), ("core", 2), ("x", 0)):
        size, have = lax.axis_size(name), 1
        per = gathered.shape[0]
        unit = (np.arange(3) == axis).astype(np.int32)[:, None]
        while have < size:
            extra = min(have, size - have)
            coming = lax.ppermute(
                gathered[: extra * per],
                name,
                [(sender, (sender + have) % size) for sender in range(size)],
            )
            gathered = jnp.concatenate([gathered, coming], axis=0)
            offsets = np.concatenate([offsets, offsets[:, : extra * per] + have * unit], axis=1)
            have += extra
    spots = [
        (lax.axis_index(name) + lax.axis_size(name) - offsets[axis]) % lax.axis_size(name)
        for axis, name in enumerate(("x", "z", "core"))
    ]
    row_ids = ((spots[0] * nz + spots[1]) * ncore + spots[2]).astype(jnp.float32)
    map_rows = exchange(map_weight.reshape(nchan, -1, cols_dev), "chan")

    scaled = (features.astype(jnp.float32) * styles[:, None, None, :]).astype(jnp.bfloat16)
    weight_sq = jnp.sum(jnp.square(conv_weight.astype(jnp.float32)), axis=0)
    style_sq = styles * styles
    demodulate = lax.rsqrt(jnp.dot(style_sq, weight_sq, precision=highest) + 1e-08)
    padded = jnp.pad(scaled, ((0, 0), (1, 1), (1, 1), (0, 0)))
    patches = jnp.concatenate(
        [
            tap_window(padded, tap // 3, tap % 3, side_len).reshape(pixels, channels)
            for tap in range(KTAPS)
        ],
        axis=1,
    )
    weight_flat = conv_weight.reshape(KTAPS * channels, cols_dev)
    conv_out = jnp.dot(patches, weight_flat, preferred_element_type=jnp.float32)
    grad_wide = grad_out.astype(jnp.float32).reshape(pixels, cols_dev)
    demod_grad = jnp.sum(grad_wide * conv_out, axis=0, keepdims=True)
    square_grad = -0.5 * demodulate**3 * demod_grad
    grad_scaled = (grad_wide * demodulate).astype(jnp.bfloat16)
    grad_padded = jnp.pad(
        grad_scaled.reshape(samples, side_len, side_len, cols_dev), ((0, 0), (1, 1), (1, 1), (0, 0))
    )
    inner_part = jnp.zeros((pixels, channels), jnp.float32)
    for tap in range(KTAPS):
        inner_part = inner_part + lax.dot_general(
            tap_window(grad_padded, 2 - tap // 3, 2 - tap % 3, side_len).reshape(pixels, cols_dev),
            conv_weight[tap],
            (((1,), (1,)), ((), ())),
            preferred_element_type=jnp.float32,
        )
    style_part = jnp.sum(
        inner_part * features.reshape(pixels, channels).astype(jnp.float32), axis=0
    ) + (2.0 * styles * jnp.dot(square_grad, weight_sq.T, precision=highest)).reshape(channels)

    grad_inner = lax.psum_scatter(inner_part, "chan", scatter_dimension=1, tiled=True)
    style_cols = lax.dynamic_slice_in_dim(styles, chan_id * cols_dev, cols_dev, 1)
    grad_input = (grad_inner * style_cols).astype(jnp.bfloat16)

    source = jnp.where(crossover <= LAYER, partner, dp_id).astype(jnp.float32)
    tile = jnp.concatenate(
        [
            style_part.reshape(1, -1, LANES),
            jnp.broadcast_to(source[:, None, None], (1, 8, LANES)),
        ],
        axis=1,
    )
    tile, map_rows = lax.optimization_barrier((tile, map_rows))
    parts = exchange(
        jnp.broadcast_to(tile, (ncore * nchan,) + tile.shape[1:]), ("core", "chan")
    ).reshape(ncore, nchan, -1, LANES)
    style_grad = jnp.sum(parts[:, :, :-8], axis=1)
    source = parts[:, 0, -1]
    hidden_cols = jnp.sum(
        lax.dot_general(
            map_rows,
            style_grad.reshape(ncore, nchan, cols_dev),
            (((2,), (2,)), ((0,), (1,))),
            precision=highest,
        ),
        axis=0,
    ).T
    style_own = lax.dynamic_slice_in_dim(
        style_grad.reshape(ncore, nchan, cols_dev), chan_id, 1, 1
    ).reshape(ncore, cols_dev)

    style_factor = jnp.dot(style_sq.T, square_grad, precision=highest)
    product_rows = lax.dot_general(
        patches, grad_scaled, (((0,), (0,)), ((), ())), preferred_element_type=jnp.float32
    ) + 2.0 * weight_flat.astype(jnp.float32) * jnp.tile(style_factor, (KTAPS, 1))
    pieces = product_rows.reshape(nx * nz, ncore, rows_dev, cols_dev).transpose(1, 0, 2, 3)
    pieces, parts = lax.optimization_barrier((pieces, parts))
    pieces = jnp.sum(exchange(pieces, "core"), axis=0)
    pieces = pieces.reshape(nx, nz * rows_dev, cols_dev)
    pad_rows = jnp.zeros((8 - 3 * ncore, cols_dev), jnp.float32)
    riders = jnp.concatenate([style_own, hidden_cols, source, pad_rows], axis=0)
    moved = exchange(
        jnp.concatenate([pieces, jnp.broadcast_to(riders[None], (nx,) + riders.shape)], axis=1), "x"
    )
    pieces = jnp.sum(moved[:, : nz * rows_dev], axis=0).reshape(nz, rows_dev, cols_dev)
    riders = jnp.concatenate(
        [
            moved[:, nz * rows_dev + kind * ncore : nz * rows_dev + (kind + 1) * ncore].reshape(
                nx * ncore, cols_dev
            )
            for kind in range(3)
        ],
        axis=0,
    )
    moved = exchange(
        jnp.concatenate([pieces, jnp.broadcast_to(riders[None], (nz,) + riders.shape)], axis=1), "z"
    )
    grad_weight = jnp.sum(moved[:, :rows_dev], axis=0) / batch_size

    per = nx * ncore
    style_all, hidden_all, source_all = (
        moved[:, rows_dev + kind * per : rows_dev + (kind + 1) * per].reshape(batch_size, cols_dev)
        for kind in range(3)
    )
    matches = (
        source_all[:, :1] == row_ids[None, :]
    ).astype(jnp.float32)
    received = lax.dot_general(
        matches,
        jnp.concatenate([style_all, hidden_all], axis=1),
        (((0,), (0,)), ((), ())),
        precision=highest,
    )
    incoming, hidden_grad = received[:, :cols_dev], received[:, cols_dev:]
    half = channels // LANES
    all_latents = gathered[:, :half].reshape(batch_size, -1)
    all_pre = gathered[:, half:].reshape(batch_size, -1)
    hidden = jnp.where(all_pre > 0, all_pre, 0.2 * all_pre)
    grad_map_out = (
        lax.dot_general(hidden, incoming, (((0,), (0,)), ((), ())), precision=highest) / batch_size
    )
    pre_cols = lax.dynamic_slice_in_dim(all_pre, chan_id * cols_dev, cols_dev, 1)
    pre_grad = hidden_grad * jnp.where(pre_cols > 0, 1.0, 0.2)
    grad_map_in = (
        lax.dot_general(all_latents, pre_grad, (((0,), (0,)), ((), ())), precision=highest)
        / batch_size
    )
    return (
        grad_weight,
        grad_input.reshape(samples, side_len, side_len, cols_dev),
        grad_map_out,
        grad_map_in,
    )


def solution(mesh):
    dp_count, chan_count = mesh.devices.shape
    split = Mesh(
        mesh.devices.reshape(dp_axes(dp_count) + (chan_count,)), ("x", "z", "core", "chan")
    )
    dp = ("x", "z", "core")
    in_specs = (
        P(dp, None, None, None),
        P(dp, None),
        P(None, None, "chan"),
        P(dp, None, None, "chan"),
        P(dp),
        P(dp),
        P(dp, None),
        P(dp, None),
        P(None, "chan"),
    )
    out_specs = (P(dp, "chan"), P(dp, None, None, "chan"), P(None, "chan"), P(None, "chan"))
    return jax.shard_map(local, mesh=split, in_specs=in_specs, out_specs=out_specs, check_vma=False)
```

```python
import jax
import jax.numpy as jnp
import numpy as np
from jax import lax
from jax.sharding import Mesh, PartitionSpec as P

KTAPS = 9
LAYER = 6
LANES = 128

highest = lax.Precision.HIGHEST


def dp_axes(dp_count):
    return (4, 12, 2) if dp_count == 96 else (2, dp_count // 4, 2)


def tap_window(padded, row_off, col_off, side_len):
    return padded[:, row_off : row_off + side_len, col_off : col_off + side_len, :]


def doubled(rows, name, have):
    size = lax.axis_size(name)
    extra = min(have, size - have)
    per = rows.shape[0] // have
    coming = lax.ppermute(
        rows[: extra * per], name, [(sender, (sender + have) % size) for sender in range(size)]
    )
    return jnp.concatenate([rows, coming], axis=0)


def flipped_sum(rows, bit):
    size = lax.axis_size("chan")
    return rows + lax.ppermute(rows, "chan", [(sender, sender ^ bit) for sender in range(size)])


def exchange(blocks, axes):
    return lax.all_to_all(blocks, axes, 0, 0, tiled=True)


def local(
    features, styles, conv_weight, grad_out, crossover, partner, latents, map_pre, map_weight
):
    samples, side_len, _, channels = features.shape
    cols_dev = conv_weight.shape[2]
    pixels = samples * side_len * side_len
    nx, nz, ncore, nchan = (lax.axis_size(name) for name in ("x", "z", "core", "chan"))
    batch_size = nx * nz * ncore
    rows_dev = KTAPS * channels // batch_size
    chan_id = lax.axis_index("chan")
    dp_id = (lax.axis_index("x") * nz + lax.axis_index("z")) * ncore + lax.axis_index("core")

    own_rows = jnp.concatenate(
        [latents.reshape(1, -1, LANES), map_pre.reshape(1, -1, LANES)], axis=1
    )
    rows_z2 = doubled(own_rows, "z", 1)
    map_rows = exchange(map_weight.reshape(nchan, -1, cols_dev), "chan")

    scaled = (features.astype(jnp.float32) * styles[:, None, None, :]).astype(jnp.bfloat16)
    weight_sq = jnp.sum(jnp.square(conv_weight.astype(jnp.float32)), axis=0)
    style_sq = styles * styles
    demodulate = lax.rsqrt(jnp.dot(style_sq, weight_sq, precision=highest) + 1e-08)
    padded = jnp.pad(scaled, ((0, 0), (1, 1), (1, 1), (0, 0)))
    patches = jnp.concatenate(
        [
            tap_window(padded, tap // 3, tap % 3, side_len).reshape(pixels, channels)
            for tap in range(KTAPS)
        ],
        axis=1,
    )
    weight_flat = conv_weight.reshape(KTAPS * channels, cols_dev)
    conv_out = jnp.dot(patches, weight_flat, preferred_element_type=jnp.float32)
    grad_wide = grad_out.astype(jnp.float32).reshape(pixels, cols_dev)
    demod_grad = jnp.sum(grad_wide * conv_out, axis=0, keepdims=True)
    square_grad = -0.5 * demodulate**3 * demod_grad
    grad_scaled = (grad_wide * demodulate).astype(jnp.bfloat16)
    grad_padded = jnp.pad(
        grad_scaled.reshape(samples, side_len, side_len, cols_dev), ((0, 0), (1, 1), (1, 1), (0, 0))
    )
    inner_part = jnp.zeros((pixels, channels), jnp.float32)
    for tap in range(KTAPS):
        inner_part = inner_part + lax.dot_general(
            tap_window(grad_padded, 2 - tap // 3, 2 - tap % 3, side_len).reshape(pixels, cols_dev),
            conv_weight[tap],
            (((1,), (1,)), ((), ())),
            preferred_element_type=jnp.float32,
        )
    style_part = jnp.sum(
        inner_part * features.reshape(pixels, channels).astype(jnp.float32), axis=0
    ) + (2.0 * styles * jnp.dot(square_grad, weight_sq.T, precision=highest)).reshape(channels)

    grad_inner = lax.psum_scatter(inner_part, "chan", scatter_dimension=1, tiled=True)
    style_cols = lax.dynamic_slice_in_dim(styles, chan_id * cols_dev, cols_dev, 1)
    grad_input = (grad_inner * style_cols).astype(jnp.bfloat16)

    style_factor = jnp.dot(style_sq.T, square_grad, precision=highest)
    product_rows = lax.dot_general(
        patches, grad_scaled, (((0,), (0,)), ((), ())), preferred_element_type=jnp.float32
    ) + 2.0 * weight_flat.astype(jnp.float32) * jnp.tile(style_factor, (KTAPS, 1))
    pieces = product_rows.reshape(nx * nz, ncore, rows_dev, cols_dev).transpose(1, 0, 2, 3)
    tile = style_part.reshape(channels // LANES, LANES)
    pieces, tile, map_rows, rows_z2 = lax.optimization_barrier((pieces, tile, map_rows, rows_z2))
    pieces = jnp.sum(exchange(pieces, "core"), axis=0).reshape(nx, nz * rows_dev, cols_dev)
    tile = flipped_sum(tile, 1)
    rows_z4 = doubled(rows_z2, "z", 2)
    pieces, tile, rows_z4 = lax.optimization_barrier((pieces, tile, rows_z4))
    pieces = jnp.sum(exchange(pieces, "x"), axis=0).reshape(nz, rows_dev, cols_dev)
    bit = 2
    while bit < nchan:
        tile = flipped_sum(tile, bit)
        bit *= 2
    hidden_row = jnp.sum(
        lax.dot_general(
            map_rows,
            tile.reshape(nchan, cols_dev),
            (((2,), (1,)), ((0,), (0,))),
            precision=highest,
        ),
        axis=0,
        keepdims=True,
    )
    style_row = lax.dynamic_slice_in_dim(tile.reshape(nchan, cols_dev), chan_id, 1, 0)
    source = jnp.where(crossover <= LAYER, partner, dp_id).astype(jnp.float32)
    own = (style_row, hidden_row, jnp.broadcast_to(source[:, None], (1, cols_dev)))
    others = lax.ppermute(
        jnp.concatenate(own + (jnp.zeros((5, cols_dev), jnp.float32),), axis=0),
        "core",
        [(core, (core + 1) % ncore) for core in range(ncore)],
    )
    chip = jnp.concatenate(
        [part for kind in range(3) for part in (own[kind], others[kind : kind + 1])]
        + [jnp.zeros((2, cols_dev), jnp.float32)],
        axis=0,
    )
    chips = [chip] + [
        lax.ppermute(chip, "x", [(sender, (sender + hop) % nx) for sender in range(nx)])
        for hop in range(1, nx)
    ]
    riders = jnp.concatenate(
        [one[kind * ncore : (kind + 1) * ncore] for kind in range(3) for one in chips], axis=0
    )
    have = 4
    rows_z = rows_z4
    while have < nz:
        rows_z = doubled(rows_z, "z", have)
        have = min(2 * have, nz)
    pieces, riders, rows_z = lax.optimization_barrier((pieces, riders, rows_z))
    moved = exchange(
        jnp.concatenate([pieces, jnp.broadcast_to(riders[None], (nz,) + riders.shape)], axis=1), "z"
    )
    gathered = doubled(rows_z, "core", 1)
    have = 1
    while have < nx:
        gathered = doubled(gathered, "x", have)
        have *= 2
    back_x, back_core, back_z = np.meshgrid(
        np.arange(nx), np.arange(ncore), np.arange(nz), indexing="ij"
    )
    spots = [
        (lax.axis_index(name) + lax.axis_size(name) - back.reshape(-1)) % lax.axis_size(name)
        for name, back in (("x", back_x), ("z", back_z), ("core", back_core))
    ]
    row_ids = ((spots[0] * nz + spots[1]) * ncore + spots[2]).astype(jnp.float32)
    grad_weight = jnp.sum(moved[:, :rows_dev], axis=0) / batch_size

    per = nx * ncore
    style_all, hidden_all, source_all = (
        moved[:, rows_dev + kind * per : rows_dev + (kind + 1) * per].reshape(batch_size, cols_dev)
        for kind in range(3)
    )
    matches = (
        source_all[:, :1] == row_ids[None, :]
    ).astype(jnp.float32)
    received = lax.dot_general(
        matches,
        jnp.concatenate([style_all, hidden_all], axis=1),
        (((0,), (0,)), ((), ())),
        precision=highest,
    )
    incoming, hidden_grad = received[:, :cols_dev], received[:, cols_dev:]
    half = channels // LANES
    all_latents = gathered[:, :half].reshape(batch_size, -1)
    all_pre = gathered[:, half:].reshape(batch_size, -1)
    hidden = jnp.where(all_pre > 0, all_pre, 0.2 * all_pre)
    grad_map_out = (
        lax.dot_general(hidden, incoming, (((0,), (0,)), ((), ())), precision=highest) / batch_size
    )
    pre_cols = lax.dynamic_slice_in_dim(all_pre, chan_id * cols_dev, cols_dev, 1)
    pre_grad = hidden_grad * jnp.where(pre_cols > 0, 1.0, 0.2)
    grad_map_in = (
        lax.dot_general(all_latents, pre_grad, (((0,), (0,)), ((), ())), precision=highest)
        / batch_size
    )
    return (
        grad_weight,
        grad_input.reshape(samples, side_len, side_len, cols_dev),
        grad_map_out,
        grad_map_in,
    )


def solution(mesh):
    dp_count, chan_count = mesh.devices.shape
    split = Mesh(
        mesh.devices.reshape(dp_axes(dp_count) + (chan_count,)), ("x", "z", "core", "chan")
    )
    dp = ("x", "z", "core")
    in_specs = (
        P(dp, None, None, None),
        P(dp, None),
        P(None, None, "chan"),
        P(dp, None, None, "chan"),
        P(dp),
        P(dp),
        P(dp, None),
        P(dp, None),
        P(None, "chan"),
    )
    out_specs = (P(dp, "chan"), P(dp, None, None, "chan"), P(None, "chan"), P(None, "chan"))
    return jax.shard_map(local, mesh=split, in_specs=in_specs, out_specs=out_specs, check_vma=False)
```

```python
import jax
import jax.numpy as jnp
import numpy as np
from jax import lax
from jax.sharding import Mesh, PartitionSpec as P

KTAPS = 9
LAYER = 6
LANES = 128

highest = lax.Precision.HIGHEST


def dp_axes(dp_count):
    return (4, 12, 2) if dp_count == 96 else (2, dp_count // 4, 2)


def tap_window(padded, row_off, col_off, side_len):
    return padded[:, row_off : row_off + side_len, col_off : col_off + side_len, :]


def doubled(rows, name, have):
    size = lax.axis_size(name)
    extra = min(have, size - have)
    per = rows.shape[0] // have
    coming = lax.ppermute(
        rows[: extra * per], name, [(sender, (sender + have) % size) for sender in range(size)]
    )
    return jnp.concatenate([rows, coming], axis=0)


def exchange(blocks, axes):
    return lax.all_to_all(blocks, axes, 0, 0, tiled=True)


def local(
    features, styles, conv_weight, grad_out, crossover, partner, latents, map_pre, map_weight
):
    samples, side_len, _, channels = features.shape
    cols_dev = conv_weight.shape[2]
    pixels = samples * side_len * side_len
    nx, nz, ncore, nchan = (lax.axis_size(name) for name in ("x", "z", "core", "chan"))
    batch_size = nx * nz * ncore
    rows_dev = KTAPS * channels // batch_size
    chan_id = lax.axis_index("chan")
    dp_id = (lax.axis_index("x") * nz + lax.axis_index("z")) * ncore + lax.axis_index("core")

    own_rows = jnp.concatenate(
        [latents.reshape(1, -1, LANES), map_pre.reshape(1, -1, LANES)], axis=1
    )
    rows_z2 = doubled(own_rows, "z", 1)
    map_rows = exchange(map_weight.reshape(nchan, -1, cols_dev), "chan")

    scaled = (features.astype(jnp.float32) * styles[:, None, None, :]).astype(jnp.bfloat16)
    weight_sq = jnp.sum(jnp.square(conv_weight.astype(jnp.float32)), axis=0)
    style_sq = styles * styles
    demodulate = lax.rsqrt(jnp.dot(style_sq, weight_sq, precision=highest) + 1e-08)
    padded = jnp.pad(scaled, ((0, 0), (1, 1), (1, 1), (0, 0)))
    patches = jnp.concatenate(
        [
            tap_window(padded, tap // 3, tap % 3, side_len).reshape(pixels, channels)
            for tap in range(KTAPS)
        ],
        axis=1,
    )
    weight_flat = conv_weight.reshape(KTAPS * channels, cols_dev)
    conv_out = jnp.dot(patches, weight_flat, preferred_element_type=jnp.float32)
    grad_wide = grad_out.astype(jnp.float32).reshape(pixels, cols_dev)
    demod_grad = jnp.sum(grad_wide * conv_out, axis=0, keepdims=True)
    square_grad = -0.5 * demodulate**3 * demod_grad
    grad_scaled = (grad_wide * demodulate).astype(jnp.bfloat16)
    grad_padded = jnp.pad(
        grad_scaled.reshape(samples, side_len, side_len, cols_dev), ((0, 0), (1, 1), (1, 1), (0, 0))
    )
    inner_part = jnp.zeros((pixels, channels), jnp.float32)
    for tap in range(KTAPS):
        inner_part = inner_part + lax.dot_general(
            tap_window(grad_padded, 2 - tap // 3, 2 - tap % 3, side_len).reshape(pixels, cols_dev),
            conv_weight[tap],
            (((1,), (1,)), ((), ())),
            preferred_element_type=jnp.float32,
        )
    style_part = jnp.sum(
        inner_part * features.reshape(pixels, channels).astype(jnp.float32), axis=0
    ) + (2.0 * styles * jnp.dot(square_grad, weight_sq.T, precision=highest)).reshape(channels)

    grad_inner = lax.psum_scatter(inner_part, "chan", scatter_dimension=1, tiled=True)
    style_cols = lax.dynamic_slice_in_dim(styles, chan_id * cols_dev, cols_dev, 1)
    grad_input = (grad_inner * style_cols).astype(jnp.bfloat16)

    style_factor = jnp.dot(style_sq.T, square_grad, precision=highest)
    product_rows = lax.dot_general(
        patches, grad_scaled, (((0,), (0,)), ((), ())), preferred_element_type=jnp.float32
    ) + 2.0 * weight_flat.astype(jnp.float32) * jnp.tile(style_factor, (KTAPS, 1))
    source = jnp.where(crossover <= LAYER, partner, dp_id).astype(jnp.float32)
    tile = jnp.concatenate(
        [
            style_part.reshape(-1, LANES),
            jnp.broadcast_to(source[:, None], (8, LANES)),
        ],
        axis=0,
    )
    tile, product_rows, map_rows, rows_z2 = lax.optimization_barrier(
        (tile, product_rows, map_rows, rows_z2)
    )
    parts = exchange(
        jnp.broadcast_to(tile[None], (ncore * nchan,) + tile.shape), ("core", "chan")
    ).reshape(ncore, nchan, -1, LANES)
    pieces = product_rows.reshape(nx, nz, ncore, rows_dev, cols_dev)
    core_id = lax.axis_index("core")
    coming = lax.ppermute(
        lax.dynamic_index_in_dim(pieces, ncore - 1 - core_id, 2, keepdims=False),
        "core",
        [(core, ncore - 1 - core) for core in range(ncore)],
    )
    rows_z4 = doubled(rows_z2, "z", 2)
    style_grad = jnp.sum(parts[:, :, :-8], axis=1)
    hidden_rows = jnp.sum(
        lax.dot_general(
            map_rows,
            style_grad.reshape(ncore, nchan, cols_dev),
            (((2,), (2,)), ((0,), (1,))),
            precision=highest,
        ),
        axis=0,
    ).T
    style_rows = lax.dynamic_slice_in_dim(
        style_grad.reshape(ncore, nchan, cols_dev), chan_id, 1, 1
    ).reshape(ncore, cols_dev)
    riders = jnp.concatenate(
        [style_rows, hidden_rows, parts[:, 0, -1], jnp.zeros((8 - 3 * ncore, cols_dev))], axis=0
    )
    coming, riders, rows_z4 = lax.optimization_barrier((coming, riders, rows_z4))
    pieces = lax.dynamic_index_in_dim(pieces, core_id, 2, keepdims=False) + coming
    moved = exchange(
        jnp.concatenate(
            [
                pieces.reshape(nx, nz * rows_dev, cols_dev),
                jnp.broadcast_to(riders[None], (nx,) + riders.shape),
            ],
            axis=1,
        ),
        "x",
    )
    have = 4
    rows_z = rows_z4
    while have < nz:
        rows_z = doubled(rows_z, "z", have)
        have = min(2 * have, nz)
    pieces = jnp.sum(moved[:, : nz * rows_dev], axis=0).reshape(nz, rows_dev, cols_dev)
    riders = jnp.concatenate(
        [
            moved[:, nz * rows_dev + kind * ncore : nz * rows_dev + (kind + 1) * ncore].reshape(
                nx * ncore, cols_dev
            )
            for kind in range(3)
        ],
        axis=0,
    )
    pieces, riders, rows_z = lax.optimization_barrier((pieces, riders, rows_z))
    moved = exchange(
        jnp.concatenate([pieces, jnp.broadcast_to(riders[None], (nz,) + riders.shape)], axis=1), "z"
    )
    gathered = doubled(rows_z, "core", 1)
    have = 1
    while have < nx:
        gathered = doubled(gathered, "x", have)
        have *= 2
    back_x, back_core, back_z = np.meshgrid(
        np.arange(nx), np.arange(ncore), np.arange(nz), indexing="ij"
    )
    spots = [
        (lax.axis_index(name) + lax.axis_size(name) - back.reshape(-1)) % lax.axis_size(name)
        for name, back in (("x", back_x), ("z", back_z), ("core", back_core))
    ]
    row_ids = ((spots[0] * nz + spots[1]) * ncore + spots[2]).astype(jnp.float32)
    grad_weight = jnp.sum(moved[:, :rows_dev], axis=0) / batch_size

    per = nx * ncore
    style_all, hidden_all, source_all = (
        moved[:, rows_dev + kind * per : rows_dev + (kind + 1) * per].reshape(batch_size, cols_dev)
        for kind in range(3)
    )
    matches = (
        source_all[:, :1] == row_ids[None, :]
    ).astype(jnp.float32)
    received = lax.dot_general(
        matches,
        jnp.concatenate([style_all, hidden_all], axis=1),
        (((0,), (0,)), ((), ())),
        precision=highest,
    )
    incoming, hidden_grad = received[:, :cols_dev], received[:, cols_dev:]
    half = channels // LANES
    all_latents = gathered[:, :half].reshape(batch_size, -1)
    all_pre = gathered[:, half:].reshape(batch_size, -1)
    hidden = jnp.where(all_pre > 0, all_pre, 0.2 * all_pre)
    grad_map_out = (
        lax.dot_general(hidden, incoming, (((0,), (0,)), ((), ())), precision=highest) / batch_size
    )
    pre_cols = lax.dynamic_slice_in_dim(all_pre, chan_id * cols_dev, cols_dev, 1)
    pre_grad = hidden_grad * jnp.where(pre_cols > 0, 1.0, 0.2)
    grad_map_in = (
        lax.dot_general(all_latents, pre_grad, (((0,), (0,)), ((), ())), precision=highest)
        / batch_size
    )
    return (
        grad_weight,
        grad_input.reshape(samples, side_len, side_len, cols_dev),
        grad_map_out,
        grad_map_in,
    )


def solution(mesh):
    dp_count, chan_count = mesh.devices.shape
    split = Mesh(
        mesh.devices.reshape(dp_axes(dp_count) + (chan_count,)), ("x", "z", "core", "chan")
    )
    dp = ("x", "z", "core")
    in_specs = (
        P(dp, None, None, None),
        P(dp, None),
        P(None, None, "chan"),
        P(dp, None, None, "chan"),
        P(dp),
        P(dp),
        P(dp, None),
        P(dp, None),
        P(None, "chan"),
    )
    out_specs = (P(dp, "chan"), P(dp, None, None, "chan"), P(None, "chan"), P(None, "chan"))
    return jax.shard_map(local, mesh=split, in_specs=in_specs, out_specs=out_specs, check_vma=False)
```

```python
import jax
import jax.numpy as jnp
import numpy as np
from jax import lax
from jax.sharding import Mesh, PartitionSpec as P

KTAPS = 9
LAYER = 6
LANES = 128

highest = lax.Precision.HIGHEST


def dp_axes(dp_count):
    return (4, 12, 2) if dp_count == 96 else (2, dp_count // 4, 2)


def tap_window(padded, row_off, col_off, side_len):
    return padded[:, row_off : row_off + side_len, col_off : col_off + side_len, :]


def doubled(rows, name, have):
    size = lax.axis_size(name)
    extra = min(have, size - have)
    per = rows.shape[0] // have
    coming = lax.ppermute(
        rows[: extra * per], name, [(sender, (sender + have) % size) for sender in range(size)]
    )
    return jnp.concatenate([rows, coming], axis=0)


def halved(blocks, bit):
    side = (lax.axis_index("chan") // bit) % 2
    pairs = blocks.reshape((-1, 2) + blocks.shape[1:])
    coming = lax.ppermute(
        lax.dynamic_index_in_dim(pairs, 1 - side, 1, keepdims=False),
        "chan",
        [(sender, sender ^ bit) for sender in range(lax.axis_size("chan"))],
    )
    return lax.dynamic_index_in_dim(pairs, side, 1, keepdims=False) + coming


def exchange(blocks, axes):
    return lax.all_to_all(blocks, axes, 0, 0, tiled=True)


def local(
    features, styles, conv_weight, grad_out, crossover, partner, latents, map_pre, map_weight
):
    samples, side_len, _, channels = features.shape
    cols_dev = conv_weight.shape[2]
    pixels = samples * side_len * side_len
    nx, nz, ncore, nchan = (lax.axis_size(name) for name in ("x", "z", "core", "chan"))
    batch_size = nx * nz * ncore
    rows_dev = KTAPS * channels // batch_size
    chan_id = lax.axis_index("chan")
    dp_id = (lax.axis_index("x") * nz + lax.axis_index("z")) * ncore + lax.axis_index("core")

    own_rows = jnp.concatenate(
        [latents.reshape(1, -1, LANES), map_pre.reshape(1, -1, LANES)], axis=1
    )
    rows_z2 = doubled(own_rows, "z", 1)
    map_rows = exchange(map_weight.reshape(nchan, -1, cols_dev), "chan")

    scaled = (features.astype(jnp.float32) * styles[:, None, None, :]).astype(jnp.bfloat16)
    weight_sq = jnp.sum(jnp.square(conv_weight.astype(jnp.float32)), axis=0)
    style_sq = styles * styles
    demodulate = lax.rsqrt(jnp.dot(style_sq, weight_sq, precision=highest) + 1e-08)
    padded = jnp.pad(scaled, ((0, 0), (1, 1), (1, 1), (0, 0)))
    patches = jnp.concatenate(
        [
            tap_window(padded, tap // 3, tap % 3, side_len).reshape(pixels, channels)
            for tap in range(KTAPS)
        ],
        axis=1,
    )
    weight_flat = conv_weight.reshape(KTAPS * channels, cols_dev)
    conv_out = jnp.dot(patches, weight_flat, preferred_element_type=jnp.float32)
    grad_wide = grad_out.astype(jnp.float32).reshape(pixels, cols_dev)
    demod_grad = jnp.sum(grad_wide * conv_out, axis=0, keepdims=True)
    square_grad = -0.5 * demodulate**3 * demod_grad
    grad_scaled = (grad_wide * demodulate).astype(jnp.bfloat16)
    grad_padded = jnp.pad(
        grad_scaled.reshape(samples, side_len, side_len, cols_dev), ((0, 0), (1, 1), (1, 1), (0, 0))
    )
    inner_part = jnp.zeros((pixels, channels), jnp.float32)
    for tap in range(KTAPS):
        inner_part = inner_part + lax.dot_general(
            tap_window(grad_padded, 2 - tap // 3, 2 - tap % 3, side_len).reshape(pixels, cols_dev),
            conv_weight[tap],
            (((1,), (1,)), ((), ())),
            preferred_element_type=jnp.float32,
        )
    style_part = jnp.sum(
        inner_part * features.reshape(pixels, channels).astype(jnp.float32), axis=0
    ) + (2.0 * styles * jnp.dot(square_grad, weight_sq.T, precision=highest)).reshape(channels)

    inner_part = inner_part.reshape(pixels, nchan, cols_dev).transpose(1, 0, 2)

    style_factor = jnp.dot(style_sq.T, square_grad, precision=highest)
    product_rows = lax.dot_general(
        patches, grad_scaled, (((0,), (0,)), ((), ())), preferred_element_type=jnp.float32
    ) + 2.0 * weight_flat.astype(jnp.float32) * jnp.tile(style_factor, (KTAPS, 1))
    source = jnp.where(crossover <= LAYER, partner, dp_id).astype(jnp.float32)
    tile = jnp.concatenate(
        [
            style_part.reshape(-1, LANES),
            jnp.broadcast_to(source[:, None], (8, LANES)),
        ],
        axis=0,
    )
    tile, map_rows, rows_z2 = lax.optimization_barrier((tile, map_rows, rows_z2))
    parts = exchange(
        jnp.broadcast_to(tile[None], (ncore * nchan,) + tile.shape), ("core", "chan")
    ).reshape(ncore, nchan, -1, LANES)
    pieces = product_rows.reshape(nx, nz, ncore, rows_dev, cols_dev)
    core_id = lax.axis_index("core")
    coming = lax.ppermute(
        lax.dynamic_index_in_dim(pieces, ncore - 1 - core_id, 2, keepdims=False),
        "core",
        [(core, ncore - 1 - core) for core in range(ncore)],
    )
    rows_z4 = doubled(rows_z2, "z", 2)
    style_grad = jnp.sum(parts[:, :, :-8], axis=1)
    hidden_rows = jnp.sum(
        lax.dot_general(
            map_rows,
            style_grad.reshape(ncore, nchan, cols_dev),
            (((2,), (2,)), ((0,), (1,))),
            precision=highest,
        ),
        axis=0,
    ).T
    style_rows = lax.dynamic_slice_in_dim(
        style_grad.reshape(ncore, nchan, cols_dev), chan_id, 1, 1
    ).reshape(ncore, cols_dev)
    riders = jnp.concatenate(
        [style_rows, hidden_rows, parts[:, 0, -1], jnp.zeros((8 - 3 * ncore, cols_dev))], axis=0
    )
    coming, riders, rows_z4, inner_part = lax.optimization_barrier(
        (coming, riders, rows_z4, inner_part)
    )
    pieces = lax.dynamic_index_in_dim(pieces, core_id, 2, keepdims=False) + coming
    moved = exchange(
        jnp.concatenate(
            [
                pieces.reshape(nx, nz * rows_dev, cols_dev),
                jnp.broadcast_to(riders[None], (nx,) + riders.shape),
            ],
            axis=1,
        ),
        "x",
    )
    inner_half = halved(inner_part, 1)
    have = 4
    rows_z = rows_z4
    while have < nz:
        rows_z = doubled(rows_z, "z", have)
        have = min(2 * have, nz)
    pieces = jnp.sum(moved[:, : nz * rows_dev], axis=0).reshape(nz, rows_dev, cols_dev)
    riders = jnp.concatenate(
        [
            moved[:, nz * rows_dev + kind * ncore : nz * rows_dev + (kind + 1) * ncore].reshape(
                nx * ncore, cols_dev
            )
            for kind in range(3)
        ],
        axis=0,
    )
    pieces, riders, rows_z, inner_half = lax.optimization_barrier(
        (pieces, riders, rows_z, inner_half)
    )
    moved = exchange(
        jnp.concatenate([pieces, jnp.broadcast_to(riders[None], (nz,) + riders.shape)], axis=1), "z"
    )
    gathered = doubled(rows_z, "core", 1)
    have = 1
    while have < nx:
        gathered = doubled(gathered, "x", have)
        have *= 2
    back_x, back_core, back_z = np.meshgrid(
        np.arange(nx), np.arange(ncore), np.arange(nz), indexing="ij"
    )
    spots = [
        (lax.axis_index(name) + lax.axis_size(name) - back.reshape(-1)) % lax.axis_size(name)
        for name, back in (("x", back_x), ("z", back_z), ("core", back_core))
    ]
    row_ids = ((spots[0] * nz + spots[1]) * ncore + spots[2]).astype(jnp.float32)
    bit = 2
    while bit < nchan:
        inner_half = halved(inner_half, bit)
        bit *= 2
    style_cols = lax.dynamic_slice_in_dim(styles, chan_id * cols_dev, cols_dev, 1)
    grad_input = (inner_half[0] * style_cols).astype(jnp.bfloat16)
    grad_weight = jnp.sum(moved[:, :rows_dev], axis=0) / batch_size

    per = nx * ncore
    style_all, hidden_all, source_all = (
        moved[:, rows_dev + kind * per : rows_dev + (kind + 1) * per].reshape(batch_size, cols_dev)
        for kind in range(3)
    )
    matches = (
        source_all[:, :1] == row_ids[None, :]
    ).astype(jnp.float32)
    received = lax.dot_general(
        matches,
        jnp.concatenate([style_all, hidden_all], axis=1),
        (((0,), (0,)), ((), ())),
        precision=highest,
    )
    incoming, hidden_grad = received[:, :cols_dev], received[:, cols_dev:]
    half = channels // LANES
    all_latents = gathered[:, :half].reshape(batch_size, -1)
    all_pre = gathered[:, half:].reshape(batch_size, -1)
    hidden = jnp.where(all_pre > 0, all_pre, 0.2 * all_pre)
    grad_map_out = (
        lax.dot_general(hidden, incoming, (((0,), (0,)), ((), ())), precision=lax.Precision.HIGH) / batch_size
    )
    pre_cols = lax.dynamic_slice_in_dim(all_pre, chan_id * cols_dev, cols_dev, 1)
    pre_grad = hidden_grad * jnp.where(pre_cols > 0, 1.0, 0.2)
    grad_map_in = (
        lax.dot_general(all_latents, pre_grad, (((0,), (0,)), ((), ())), precision=lax.Precision.HIGH)
        / batch_size
    )
    return (
        grad_weight,
        grad_input.reshape(samples, side_len, side_len, cols_dev),
        grad_map_out,
        grad_map_in,
    )


def solution(mesh):
    dp_count, chan_count = mesh.devices.shape
    split = Mesh(
        mesh.devices.reshape(dp_axes(dp_count) + (chan_count,)), ("x", "z", "core", "chan")
    )
    dp = ("x", "z", "core")
    in_specs = (
        P(dp, None, None, None),
        P(dp, None),
        P(None, None, "chan"),
        P(dp, None, None, "chan"),
        P(dp),
        P(dp),
        P(dp, None),
        P(dp, None),
        P(None, "chan"),
    )
    out_specs = (P(dp, "chan"), P(dp, None, None, "chan"), P(None, "chan"), P(None, "chan"))
    return jax.shard_map(local, mesh=split, in_specs=in_specs, out_specs=out_specs, check_vma=False)
```

```python
import functools

import jax
import jax.numpy as jnp
import numpy as np
from jax import lax
from jax.experimental import pallas as pl
from jax.experimental.pallas import tpu as pltpu
from jax.sharding import Mesh, PartitionSpec as P

KTAPS = 9
LAYER = 6
LANES = 128

highest = lax.Precision.HIGHEST


def dp_axes(dp_count):
    return (4, 12, 2) if dp_count == 96 else (2, dp_count // 4, 2)


def convolution_kernel(
    side, core_ref, feat_ref, style_ref, weight_ref, grad_ref, source_ref,
    sent_ref, kept_ref, inner_ref, tile_ref,
    scaled_t, shifted, product, square, factor,
):
    pixels, channels = feat_ref.shape
    cols = grad_ref.shape[1]
    block = min(256, channels)
    rows_dev = sent_ref.shape[1]
    f32, bf16 = jnp.float32, jnp.bfloat16

    for start in range(0, channels, LANES):
        total = jnp.zeros((LANES, cols), f32)
        for tap in range(KTAPS):
            wide = weight_ref[tap * channels + start : tap * channels + start + LANES].astype(f32)
            total = total + wide * wide
        square[start : start + LANES] = total
    style = style_ref[...]
    style_sq = jnp.broadcast_to(style * style, (8, channels))
    norm = jnp.dot(style_sq, square[...], precision=highest, preferred_element_type=f32)
    demodulate = lax.rsqrt(norm[:1] + 1e-08)

    grad_scaled = (grad_ref[...].astype(f32) * demodulate).astype(bf16).astype(f32)
    place = lax.broadcasted_iota(jnp.int32, (pixels, cols), 0)
    row, col = place // side, place % side
    for tap in range(KTAPS):
        down, right = tap // 3 - 1, tap % 3 - 1
        moved = grad_scaled
        if down or right:
            moved = pltpu.roll(grad_scaled, (down * side + right) % pixels, 0)
            inside = (
                (row >= down) & (row < side + down) & (col >= right) & (col < side + right)
            )
            moved = jnp.where(inside, moved, 0.0)
        shifted[:, tap * cols : (tap + 1) * cols] = moved.astype(bf16)

    demod_grad = jnp.zeros((8, cols), f32)
    for start in range(0, channels, block):
        wide = feat_ref[:, start : start + block].astype(f32) * style[:, start : start + block]
        scaled_t[start : start + block] = wide.astype(bf16).astype(f32).T.astype(bf16)
        for tap in range(0, KTAPS, 2):
            taps = min(2, KTAPS - tap)
            result = jnp.dot(
                scaled_t[start : start + block],
                shifted[:, tap * cols : (tap + taps) * cols],
                preferred_element_type=f32,
            )
            for own in range(taps):
                first = (tap + own) * channels + start
                part = result[:, own * cols : (own + 1) * cols]
                product[first : first + block] = part
                weighted = part * weight_ref[first : first + block].astype(f32)
                demod_grad = demod_grad + jnp.sum(weighted.reshape(-1, 8, cols), axis=0)
    demod_grad = jnp.sum(demod_grad, axis=0, keepdims=True) / demodulate
    square_grad = -0.5 * demodulate * demodulate * demodulate * demod_grad

    demod_part = lax.dot_general(
        jnp.broadcast_to(square_grad, (8, cols)),
        square[...],
        (((1,), (1,)), ((), ())),
        precision=highest,
        preferred_element_type=f32,
    )[:1]
    style_rows = []
    for start in range(0, channels, block):
        kernel = jnp.concatenate(
            [
                weight_ref[tap * channels + start : tap * channels + start + block]
                for tap in range(KTAPS)
            ],
            axis=1,
        )
        inner = lax.dot_general(
            shifted[...], kernel, (((1,), (1,)), ((), ())), preferred_element_type=f32
        )
        total = jnp.sum(inner * feat_ref[:, start : start + block].astype(f32), axis=0, keepdims=True)
        total = total + 2.0 * style[:, start : start + block] * demod_part[:, start : start + block]
        for own in range(block // cols):
            inner_ref[start // cols + own] = inner[:, own * cols : (own + 1) * cols]
            style_rows.append(total[:, own * cols : (own + 1) * cols])
    tile = jnp.concatenate(
        style_rows + [jnp.broadcast_to(source_ref[...], (8, cols))], axis=0
    )
    for peer in range(tile_ref.shape[0]):
        tile_ref[peer] = tile

    for start in range(0, channels, LANES):
        columns = jnp.broadcast_to(style_sq[:1, start : start + LANES], (LANES, LANES)).T
        factor[start : start + LANES] = columns * (2.0 * square_grad)

    def emit(even_ref, odd_ref):
        total = KTAPS * channels
        first = 0
        while first < total:
            chunk, at = divmod(first, rows_dev)
            source = first % channels
            size = min(rows_dev - at, channels - source)
            target = odd_ref if chunk % 2 else even_ref
            target[chunk // 2, at : at + size] = product[first : first + size] + weight_ref[
                first : first + size
            ].astype(f32) * factor[source : source + size]
            first += size

    @pl.when(core_ref[0] == 0)
    def _():
        emit(kept_ref, sent_ref)

    @pl.when(core_ref[0] != 0)
    def _():
        emit(sent_ref, kept_ref)


def convolution_part(core_id, features, styles, weight, grad_out, source, sizes):
    chunks, rows_dev, peers = sizes
    pixels, channels = features.shape
    cols = grad_out.shape[1]
    side = int(round(pixels**0.5))
    f32 = jnp.float32
    whole = pl.BlockSpec(memory_space=pltpu.VMEM)
    tile_rows = channels // LANES + 8
    return pl.pallas_call(
        functools.partial(convolution_kernel, side),
        out_shape=(
            jax.ShapeDtypeStruct((chunks, rows_dev, cols), f32),
            jax.ShapeDtypeStruct((chunks, rows_dev, cols), f32),
            jax.ShapeDtypeStruct((channels // cols, pixels, cols), f32),
            jax.ShapeDtypeStruct((peers, tile_rows, cols), f32),
        ),
        in_specs=[pl.BlockSpec(memory_space=pltpu.SMEM)] + [whole] * 5,
        out_specs=[whole] * 4,
        scratch_shapes=[
            pltpu.VMEM((channels, pixels), jnp.bfloat16),
            pltpu.VMEM((pixels, KTAPS * cols), jnp.bfloat16),
            pltpu.VMEM((KTAPS * channels, cols), f32),
            pltpu.VMEM((channels, cols), f32),
            pltpu.VMEM((channels, cols), f32),
        ],
        compiler_params=pltpu.CompilerParams(vmem_limit_bytes=32 * 1024 * 1024),
        cost_estimate=pl.CostEstimate(
            flops=4 * pixels * KTAPS * channels * cols, transcendentals=0, bytes_accessed=12_000_000
        ),
        name="convolution_part",
    )(core_id.astype(jnp.int32).reshape(1), features, styles, weight, grad_out, source)


def doubled(rows, name, have):
    size = lax.axis_size(name)
    extra = min(have, size - have)
    per = rows.shape[0] // have
    coming = lax.ppermute(
        rows[: extra * per], name, [(sender, (sender + have) % size) for sender in range(size)]
    )
    return jnp.concatenate([rows, coming], axis=0)


def halved(blocks, bit):
    side = (lax.axis_index("chan") // bit) % 2
    pairs = blocks.reshape((-1, 2) + blocks.shape[1:])
    coming = lax.ppermute(
        lax.dynamic_index_in_dim(pairs, 1 - side, 1, keepdims=False),
        "chan",
        [(sender, sender ^ bit) for sender in range(lax.axis_size("chan"))],
    )
    return lax.dynamic_index_in_dim(pairs, side, 1, keepdims=False) + coming


def exchange(blocks, axes):
    return lax.all_to_all(blocks, axes, 0, 0, tiled=True)


def local(
    features, styles, conv_weight, grad_out, crossover, partner, latents, map_pre, map_weight
):
    samples, side_len, _, channels = features.shape
    cols_dev = conv_weight.shape[2]
    pixels = samples * side_len * side_len
    nx, nz, ncore, nchan = (lax.axis_size(name) for name in ("x", "z", "core", "chan"))
    batch_size = nx * nz * ncore
    rows_dev = KTAPS * channels // batch_size
    chan_id = lax.axis_index("chan")
    dp_id = (lax.axis_index("x") * nz + lax.axis_index("z")) * ncore + lax.axis_index("core")

    own_rows = jnp.concatenate(
        [latents.reshape(1, -1, LANES), map_pre.reshape(1, -1, LANES)], axis=1
    )
    rows_z2 = doubled(own_rows, "z", 1)
    map_rows = exchange(map_weight.reshape(nchan, -1, cols_dev), "chan")

    core_id = lax.axis_index("core")
    source = jnp.where(crossover <= LAYER, partner, dp_id).astype(jnp.float32)
    sent, kept, inner_part, tile = convolution_part(
        core_id,
        features.reshape(pixels, channels),
        styles,
        conv_weight.reshape(KTAPS * channels, cols_dev),
        grad_out.reshape(pixels, cols_dev),
        jnp.broadcast_to(source[:, None], (1, cols_dev)),
        (nx * nz, rows_dev, ncore * nchan),
    )
    tile, sent, map_rows, rows_z2 = lax.optimization_barrier((tile, sent, map_rows, rows_z2))
    parts = exchange(tile, ("core", "chan")).reshape(ncore, nchan, -1, LANES)
    coming = lax.ppermute(sent, "core", [(core, ncore - 1 - core) for core in range(ncore)])
    rows_z4 = doubled(rows_z2, "z", 2)
    style_grad = jnp.sum(parts[:, :, :-8], axis=1)
    hidden_rows = jnp.sum(
        lax.dot_general(
            map_rows,
            style_grad.reshape(ncore, nchan, cols_dev),
            (((2,), (2,)), ((0,), (1,))),
            precision=highest,
        ),
        axis=0,
    ).T
    style_rows = lax.dynamic_slice_in_dim(
        style_grad.reshape(ncore, nchan, cols_dev), chan_id, 1, 1
    ).reshape(ncore, cols_dev)
    riders = jnp.concatenate(
        [style_rows, hidden_rows, parts[:, 0, -1], jnp.zeros((8 - 3 * ncore, cols_dev))], axis=0
    )
    coming, riders, rows_z4, inner_part = lax.optimization_barrier(
        (coming, riders, rows_z4, inner_part)
    )
    pieces = kept + coming
    moved = exchange(
        jnp.concatenate(
            [
                pieces.reshape(nx, nz * rows_dev, cols_dev),
                jnp.broadcast_to(riders[None], (nx,) + riders.shape),
            ],
            axis=1,
        ),
        "x",
    )
    inner_half = halved(inner_part, 1)
    have = 4
    rows_z = rows_z4
    while have < nz:
        rows_z = doubled(rows_z, "z", have)
        have = min(2 * have, nz)
    pieces = jnp.sum(moved[:, : nz * rows_dev], axis=0).reshape(nz, rows_dev, cols_dev)
    riders = jnp.concatenate(
        [
            moved[:, nz * rows_dev + kind * ncore : nz * rows_dev + (kind + 1) * ncore].reshape(
                nx * ncore, cols_dev
            )
            for kind in range(3)
        ],
        axis=0,
    )
    pieces, riders, rows_z, inner_half = lax.optimization_barrier(
        (pieces, riders, rows_z, inner_half)
    )
    moved = exchange(
        jnp.concatenate([pieces, jnp.broadcast_to(riders[None], (nz,) + riders.shape)], axis=1), "z"
    )
    inner_half = halved(inner_half, 2)
    inner_half, rows_z = lax.optimization_barrier((inner_half, rows_z))
    gathered = doubled(rows_z, "core", 1)
    have = 1
    while have < nx:
        gathered = doubled(gathered, "x", have)
        have *= 2
    back_x, back_core, back_z = np.meshgrid(
        np.arange(nx), np.arange(ncore), np.arange(nz), indexing="ij"
    )
    spots = [
        (lax.axis_index(name) + lax.axis_size(name) - back.reshape(-1)) % lax.axis_size(name)
        for name, back in (("x", back_x), ("z", back_z), ("core", back_core))
    ]
    row_ids = ((spots[0] * nz + spots[1]) * ncore + spots[2]).astype(jnp.float32)
    bit = 4
    while bit < nchan:
        inner_half = halved(inner_half, bit)
        bit *= 2
    style_cols = lax.dynamic_slice_in_dim(styles, chan_id * cols_dev, cols_dev, 1)
    grad_input = (inner_half[0] * style_cols).astype(jnp.bfloat16)
    grad_weight = jnp.sum(moved[:, :rows_dev], axis=0) / batch_size

    per = nx * ncore
    style_all, hidden_all, source_all = (
        moved[:, rows_dev + kind * per : rows_dev + (kind + 1) * per].reshape(batch_size, cols_dev)
        for kind in range(3)
    )
    matches = (
        source_all[:, :1] == row_ids[None, :]
    ).astype(jnp.float32)
    received = lax.dot_general(
        matches,
        jnp.concatenate([style_all, hidden_all], axis=1),
        (((0,), (0,)), ((), ())),
        precision=highest,
    )
    incoming, hidden_grad = received[:, :cols_dev], received[:, cols_dev:]
    half = channels // LANES
    all_latents = gathered[:, :half].reshape(batch_size, -1)
    all_pre = gathered[:, half:].reshape(batch_size, -1)
    hidden = jnp.where(all_pre > 0, all_pre, 0.2 * all_pre)
    grad_map_out = (
        lax.dot_general(hidden, incoming, (((0,), (0,)), ((), ())), precision=lax.Precision.HIGH) / batch_size
    )
    pre_cols = lax.dynamic_slice_in_dim(all_pre, chan_id * cols_dev, cols_dev, 1)
    pre_grad = hidden_grad * jnp.where(pre_cols > 0, 1.0, 0.2)
    grad_map_in = (
        lax.dot_general(all_latents, pre_grad, (((0,), (0,)), ((), ())), precision=lax.Precision.HIGH)
        / batch_size
    )
    return (
        grad_weight,
        grad_input.reshape(samples, side_len, side_len, cols_dev),
        grad_map_out,
        grad_map_in,
    )


def solution(mesh):
    dp_count, chan_count = mesh.devices.shape
    split = Mesh(
        mesh.devices.reshape(dp_axes(dp_count) + (chan_count,)), ("x", "z", "core", "chan")
    )
    dp = ("x", "z", "core")
    in_specs = (
        P(dp, None, None, None),
        P(dp, None),
        P(None, None, "chan"),
        P(dp, None, None, "chan"),
        P(dp),
        P(dp),
        P(dp, None),
        P(dp, None),
        P(None, "chan"),
    )
    out_specs = (P(dp, "chan"), P(dp, None, None, "chan"), P(None, "chan"), P(None, "chan"))
    return jax.shard_map(local, mesh=split, in_specs=in_specs, out_specs=out_specs, check_vma=False)
```

```python
import functools

import jax
import jax.numpy as jnp
import numpy as np
from jax import lax
from jax.experimental import pallas as pl
from jax.experimental.pallas import tpu as pltpu
from jax.sharding import Mesh, PartitionSpec as P

KTAPS = 9
LAYER = 6
LANES = 128

highest = lax.Precision.HIGHEST


def dp_axes(dp_count):
    return (4, 12, 2) if dp_count == 96 else (2, dp_count // 4, 2)


def convolution_kernel(
    side, rows_dev, core_ref, feat_hbm, style_hbm, weight_hbm, grad_hbm, source_ref,
    sent_hbm, kept_ref, inner_ref, tile_ref,
    feat_ref, style_ref, weight_ref, grad_ref, sent_ref,
    scaled_t, shifted, product, square, factor, in_sems, out_sems,
):
    pixels, channels = feat_ref.shape
    cols = grad_ref.shape[1]
    block = min(256, channels)
    f32, bf16 = jnp.float32, jnp.bfloat16

    arrivals = [
        pltpu.make_async_copy(source, target, in_sems.at[at])
        for at, (source, target) in enumerate(
            (
                (style_hbm, style_ref),
                (feat_hbm, feat_ref),
                (weight_hbm, weight_ref),
                (grad_hbm, grad_ref),
            )
        )
    ]
    for arrival in arrivals:
        arrival.start()
    arrivals[0].wait()
    arrivals[1].wait()
    style = style_ref[...]
    for start in range(0, channels, block):
        wide = feat_ref[:, start : start + block].astype(f32) * style[:, start : start + block]
        scaled_t[start : start + block] = wide.astype(bf16).astype(f32).T.astype(bf16)
    arrivals[2].wait()
    arrivals[3].wait()

    for start in range(0, channels, LANES):
        total = jnp.zeros((LANES, cols), f32)
        for tap in range(KTAPS):
            wide = weight_ref[tap * channels + start : tap * channels + start + LANES].astype(f32)
            total = total + wide * wide
        square[start : start + LANES] = total
    style_sq = jnp.broadcast_to(style * style, (8, channels))
    norm = jnp.dot(style_sq, square[...], precision=highest, preferred_element_type=f32)
    demodulate = lax.rsqrt(norm[:1] + 1e-08)

    grad_scaled = (grad_ref[...].astype(f32) * demodulate).astype(bf16).astype(f32)
    place = lax.broadcasted_iota(jnp.int32, (pixels, cols), 0)
    row, col = place // side, place % side
    for tap in range(KTAPS):
        down, right = tap // 3 - 1, tap % 3 - 1
        moved = grad_scaled
        if down or right:
            moved = pltpu.roll(grad_scaled, (down * side + right) % pixels, 0)
            inside = (
                (row >= down) & (row < side + down) & (col >= right) & (col < side + right)
            )
            moved = jnp.where(inside, moved, 0.0)
        shifted[:, tap * cols : (tap + 1) * cols] = moved.astype(bf16)

    demod_grad = jnp.zeros((8, cols), f32)
    for start in range(0, channels, block):
        for tap in range(0, KTAPS, 2):
            taps = min(2, KTAPS - tap)
            result = jnp.dot(
                scaled_t[start : start + block],
                shifted[:, tap * cols : (tap + taps) * cols],
                preferred_element_type=f32,
            )
            for own in range(taps):
                first = (tap + own) * channels + start
                part = result[:, own * cols : (own + 1) * cols]
                product[first : first + block] = part
                weighted = part * weight_ref[first : first + block].astype(f32)
                demod_grad = demod_grad + jnp.sum(weighted.reshape(-1, 8, cols), axis=0)
    demod_grad = jnp.sum(demod_grad, axis=0, keepdims=True) / demodulate
    square_grad = -0.5 * demodulate * demodulate * demodulate * demod_grad

    demod_part = lax.dot_general(
        jnp.broadcast_to(square_grad, (8, cols)),
        square[...],
        (((1,), (1,)), ((), ())),
        precision=highest,
        preferred_element_type=f32,
    )[:1]
    style_rows = []
    for start in range(0, channels, block):
        kernel = jnp.concatenate(
            [
                weight_ref[tap * channels + start : tap * channels + start + block]
                for tap in range(KTAPS)
            ],
            axis=1,
        )
        inner = lax.dot_general(
            shifted[...], kernel, (((1,), (1,)), ((), ())), preferred_element_type=f32
        )
        total = jnp.sum(inner * feat_ref[:, start : start + block].astype(f32), axis=0, keepdims=True)
        total = total + 2.0 * style[:, start : start + block] * demod_part[:, start : start + block]
        for own in range(block // cols):
            inner_ref[start // cols + own] = inner[:, own * cols : (own + 1) * cols]
            style_rows.append(total[:, own * cols : (own + 1) * cols])
    tile = jnp.concatenate(
        style_rows + [jnp.broadcast_to(source_ref[...], (8, cols))], axis=0
    )
    for peer in range(tile_ref.shape[0]):
        tile_ref[peer] = tile

    for start in range(0, channels, LANES):
        columns = jnp.broadcast_to(style_sq[:1, start : start + LANES], (LANES, LANES)).T
        factor[start : start + LANES] = columns * (2.0 * square_grad)

    per_row = sent_ref.shape[1] // rows_dev
    for row in range(sent_ref.shape[0]):
        for target in (sent_ref, kept_ref):
            target[row, per_row * rows_dev :] = jnp.zeros((8, cols), f32)

    ncore = 2
    departures = [
        pltpu.make_async_copy(sent_ref.at[row], sent_hbm.at[row], out_sems.at[row])
        for row in range(sent_ref.shape[0])
    ]

    def emit(even_ref, odd_ref):
        total = KTAPS * channels
        first = 0
        while first < total:
            chunk, at = divmod(first, rows_dev)
            source = first % channels
            size = min(rows_dev - at, channels - source)
            target = odd_ref if chunk % 2 else even_ref
            row, place = divmod(chunk // 2, per_row)
            at += place * rows_dev
            target[row, at : at + size] = product[first : first + size] + weight_ref[
                first : first + size
            ].astype(f32) * factor[source : source + size]
            first += size
            if first % (ncore * per_row * rows_dev) == 0:
                departures[row].start()
        for departure in departures:
            departure.wait()

    @pl.when(core_ref[0] == 0)
    def _():
        emit(kept_ref, sent_ref)

    @pl.when(core_ref[0] != 0)
    def _():
        emit(sent_ref, kept_ref)


def convolution_part(core_id, features, styles, weight, grad_out, source, sizes):
    far, near, rows_dev, peers = sizes
    pixels, channels = features.shape
    cols = grad_out.shape[1]
    side = int(round(pixels**0.5))
    f32 = jnp.float32
    whole = pl.BlockSpec(memory_space=pltpu.VMEM)
    away = pl.BlockSpec(memory_space=pltpu.HBM)
    tile_rows = channels // LANES + 8
    return pl.pallas_call(
        functools.partial(convolution_kernel, side, rows_dev),
        out_shape=(
            pltpu.HBM((far, near * rows_dev + 8, cols), f32),
            jax.ShapeDtypeStruct((far, near * rows_dev + 8, cols), f32),
            jax.ShapeDtypeStruct((channels // cols, pixels, cols), f32),
            jax.ShapeDtypeStruct((peers, tile_rows, cols), f32),
        ),
        in_specs=[pl.BlockSpec(memory_space=pltpu.SMEM)] + [away] * 4 + [whole],
        out_specs=[away] + [whole] * 3,
        scratch_shapes=[
            pltpu.VMEM((pixels, channels), jnp.bfloat16),
            pltpu.VMEM((1, channels), f32),
            pltpu.VMEM((KTAPS * channels, cols), jnp.bfloat16),
            pltpu.VMEM((pixels, cols), jnp.bfloat16),
            pltpu.VMEM((far, near * rows_dev + 8, cols), f32),
            pltpu.VMEM((channels, pixels), jnp.bfloat16),
            pltpu.VMEM((pixels, KTAPS * cols), jnp.bfloat16),
            pltpu.VMEM((KTAPS * channels, cols), f32),
            pltpu.VMEM((channels, cols), f32),
            pltpu.VMEM((channels, cols), f32),
            pltpu.SemaphoreType.DMA((4,)),
            pltpu.SemaphoreType.DMA((far,)),
        ],
        compiler_params=pltpu.CompilerParams(vmem_limit_bytes=32 * 1024 * 1024),
        cost_estimate=pl.CostEstimate(
            flops=4 * pixels * KTAPS * channels * cols, transcendentals=0, bytes_accessed=12_000_000
        ),
        name="convolution_part",
    )(
        core_id.astype(jnp.int32).reshape(1),
        *(
            pltpu.with_memory_space_constraint(one, pltpu.HBM)
            for one in (features, styles, weight, grad_out)
        ),
        source,
    )


def doubled(rows, name, have):
    size = lax.axis_size(name)
    extra = min(have, size - have)
    per = rows.shape[0] // have
    coming = lax.ppermute(
        rows[: extra * per], name, [(sender, (sender + have) % size) for sender in range(size)]
    )
    return jnp.concatenate([rows, coming], axis=0)


def halved(blocks, bit):
    side = (lax.axis_index("chan") // bit) % 2
    pairs = blocks.reshape((-1, 2) + blocks.shape[1:])
    coming = lax.ppermute(
        lax.dynamic_index_in_dim(pairs, 1 - side, 1, keepdims=False),
        "chan",
        [(sender, sender ^ bit) for sender in range(lax.axis_size("chan"))],
    )
    return lax.dynamic_index_in_dim(pairs, side, 1, keepdims=False) + coming


def exchange(blocks, axes):
    return lax.all_to_all(blocks, axes, 0, 0, tiled=True)


def local(
    features, styles, conv_weight, grad_out, crossover, partner, latents, map_pre, map_weight
):
    samples, side_len, _, channels = features.shape
    cols_dev = conv_weight.shape[2]
    pixels = samples * side_len * side_len
    nx, nz, ncore, nchan = (lax.axis_size(name) for name in ("x", "z", "core", "chan"))
    batch_size = nx * nz * ncore
    rows_dev = KTAPS * channels // batch_size
    chan_id = lax.axis_index("chan")
    dp_id = (lax.axis_index("x") * nz + lax.axis_index("z")) * ncore + lax.axis_index("core")

    own_rows = jnp.concatenate(
        [latents.reshape(1, -1, LANES), map_pre.reshape(1, -1, LANES)], axis=1
    )
    rows_z2 = doubled(own_rows, "z", 1)
    map_rows = exchange(map_weight.reshape(nchan, -1, cols_dev), "chan")

    core_id = lax.axis_index("core")
    source = jnp.where(crossover <= LAYER, partner, dp_id).astype(jnp.float32)
    sent, kept, inner_part, tile = convolution_part(
        core_id,
        features.reshape(pixels, channels),
        styles,
        conv_weight.reshape(KTAPS * channels, cols_dev),
        grad_out.reshape(pixels, cols_dev),
        jnp.broadcast_to(source[:, None], (1, cols_dev)),
        (nx, nz, rows_dev, ncore * nchan),
    )
    tile, sent, map_rows, rows_z2 = lax.optimization_barrier((tile, sent, map_rows, rows_z2))
    parts = exchange(tile, ("core", "chan")).reshape(ncore, nchan, -1, LANES)
    coming = lax.ppermute(sent, "core", [(core, ncore - 1 - core) for core in range(ncore)])
    inner_half = halved(inner_part, 1)
    style_grad = jnp.sum(parts[:, :, :-8], axis=1)
    hidden_rows = jnp.sum(
        lax.dot_general(
            map_rows,
            style_grad.reshape(ncore, nchan, cols_dev),
            (((2,), (2,)), ((0,), (1,))),
            precision=highest,
        ),
        axis=0,
    ).T
    style_rows = lax.dynamic_slice_in_dim(
        style_grad.reshape(ncore, nchan, cols_dev), chan_id, 1, 1
    ).reshape(ncore, cols_dev)
    riders = jnp.concatenate(
        [style_rows, hidden_rows, parts[:, 0, -1], jnp.zeros((8 - 3 * ncore, cols_dev))], axis=0
    )
    coming, riders, rows_z2 = lax.optimization_barrier((coming, riders, rows_z2))
    moved = exchange(
        kept
        + coming
        + jnp.pad(
            jnp.broadcast_to(riders[None], (nx,) + riders.shape),
            ((0, 0), (nz * rows_dev, 0), (0, 0)),
        ),
        "x",
    )
    rows_z, have = rows_z2, 2
    while have < nz:
        rows_z = doubled(rows_z, "z", have)
        have = min(2 * have, nz)
    gathered = doubled(rows_z, "core", 1)
    pieces = jnp.sum(moved[:, : nz * rows_dev], axis=0).reshape(nz, rows_dev, cols_dev)
    riders = jnp.concatenate(
        [
            moved[:, nz * rows_dev + kind * ncore : nz * rows_dev + (kind + 1) * ncore].reshape(
                nx * ncore, cols_dev
            )
            for kind in range(3)
        ],
        axis=0,
    )
    pieces, riders, gathered, inner_half = lax.optimization_barrier(
        (pieces, riders, gathered, inner_half)
    )
    moved = exchange(
        jnp.concatenate([pieces, jnp.broadcast_to(riders[None], (nz,) + riders.shape)], axis=1), "z"
    )
    gathered = jnp.concatenate(
        [gathered]
        + [
            lax.ppermute(gathered, "x", [(sender, (sender + hop) % nx) for sender in range(nx)])
            for hop in range(1, nx)
        ],
        axis=0,
    )
    back_x, back_core, back_z = np.meshgrid(
        np.arange(nx), np.arange(ncore), np.arange(nz), indexing="ij"
    )
    spots = [
        (lax.axis_index(name) + lax.axis_size(name) - back.reshape(-1)) % lax.axis_size(name)
        for name, back in (("x", back_x), ("z", back_z), ("core", back_core))
    ]
    row_ids = ((spots[0] * nz + spots[1]) * ncore + spots[2]).astype(jnp.float32)
    bit = 2
    while bit < nchan:
        inner_half = halved(inner_half, bit)
        bit *= 2
    style_cols = lax.dynamic_slice_in_dim(styles, chan_id * cols_dev, cols_dev, 1)
    grad_input = (inner_half[0] * style_cols).astype(jnp.bfloat16)
    grad_weight = jnp.sum(moved[:, :rows_dev], axis=0) / batch_size

    per = nx * ncore
    style_all, hidden_all, source_all = (
        moved[:, rows_dev + kind * per : rows_dev + (kind + 1) * per].reshape(batch_size, cols_dev)
        for kind in range(3)
    )
    matches = (
        source_all[:, :1] == row_ids[None, :]
    ).astype(jnp.float32)
    received = lax.dot_general(
        matches,
        jnp.concatenate([style_all, hidden_all], axis=1),
        (((0,), (0,)), ((), ())),
        precision=highest,
    )
    incoming, hidden_grad = received[:, :cols_dev], received[:, cols_dev:]
    half = channels // LANES
    all_latents = gathered[:, :half].reshape(batch_size, -1)
    all_pre = gathered[:, half:].reshape(batch_size, -1)
    hidden = jnp.where(all_pre > 0, all_pre, 0.2 * all_pre)
    grad_map_out = (
        lax.dot_general(hidden, incoming, (((0,), (0,)), ((), ())), precision=lax.Precision.HIGH) / batch_size
    )
    pre_cols = lax.dynamic_slice_in_dim(all_pre, chan_id * cols_dev, cols_dev, 1)
    pre_grad = hidden_grad * jnp.where(pre_cols > 0, 1.0, 0.2)
    grad_map_in = (
        lax.dot_general(all_latents, pre_grad, (((0,), (0,)), ((), ())), precision=lax.Precision.HIGH)
        / batch_size
    )
    return (
        grad_weight,
        grad_input.reshape(samples, side_len, side_len, cols_dev),
        grad_map_out,
        grad_map_in,
    )


def solution(mesh):
    dp_count, chan_count = mesh.devices.shape
    split = Mesh(
        mesh.devices.reshape(dp_axes(dp_count) + (chan_count,)), ("x", "z", "core", "chan")
    )
    dp = ("x", "z", "core")
    in_specs = (
        P(dp, None, None, None),
        P(dp, None),
        P(None, None, "chan"),
        P(dp, None, None, "chan"),
        P(dp),
        P(dp),
        P(dp, None),
        P(dp, None),
        P(None, "chan"),
    )
    out_specs = (P(dp, "chan"), P(dp, None, None, "chan"), P(None, "chan"), P(None, "chan"))
    return jax.shard_map(local, mesh=split, in_specs=in_specs, out_specs=out_specs, check_vma=False)
```

```python
import functools

import jax
import jax.numpy as jnp
import numpy as np
from jax import lax
from jax.experimental import pallas as pl
from jax.experimental.pallas import tpu as pltpu
from jax.sharding import Mesh, PartitionSpec as P

KTAPS = 9
LAYER = 6
LANES = 128

highest = lax.Precision.HIGHEST


def dp_axes(dp_count):
    return (4, 12, 2) if dp_count == 96 else (2, dp_count // 4, 2)


def convolution_kernel(
    side, rows_dev, core_ref, feat_hbm, style_hbm, weight_hbm, grad_hbm, source_ref,
    sent_hbm, kept_ref, inner_ref, tile_ref,
    feat_ref, style_ref, weight_ref, grad_ref, sent_ref,
    scaled_t, shifted, product, square, factor, in_sems, out_sems,
):
    pixels, channels = feat_ref.shape
    cols = grad_ref.shape[1]
    block = min(256, channels)
    f32, bf16 = jnp.float32, jnp.bfloat16

    arrivals = [
        pltpu.make_async_copy(source, target, in_sems.at[at])
        for at, (source, target) in enumerate(
            (
                (style_hbm, style_ref),
                (feat_hbm, feat_ref),
                (weight_hbm, weight_ref),
                (grad_hbm, grad_ref),
            )
        )
    ]
    for arrival in arrivals:
        arrival.start()
    arrivals[0].wait()
    arrivals[1].wait()
    style = style_ref[...]
    for start in range(0, channels, block):
        wide = feat_ref[:, start : start + block].astype(f32) * style[:, start : start + block]
        scaled_t[start : start + block] = wide.astype(bf16).astype(f32).T.astype(bf16)
    arrivals[2].wait()
    arrivals[3].wait()

    for start in range(0, channels, LANES):
        total = jnp.zeros((LANES, cols), f32)
        for tap in range(KTAPS):
            wide = weight_ref[tap * channels + start : tap * channels + start + LANES].astype(f32)
            total = total + wide * wide
        square[start : start + LANES] = total
    style_sq = jnp.broadcast_to(style * style, (8, channels))
    norm = jnp.dot(style_sq, square[...], precision=highest, preferred_element_type=f32)
    demodulate = lax.rsqrt(norm[:1] + 1e-08)

    grad_scaled = (grad_ref[...].astype(f32) * demodulate).astype(bf16).astype(f32)
    place = lax.broadcasted_iota(jnp.int32, (pixels, cols), 0)
    row, col = place // side, place % side
    for tap in range(KTAPS):
        down, right = tap // 3 - 1, tap % 3 - 1
        moved = grad_scaled
        if down or right:
            moved = pltpu.roll(grad_scaled, (down * side + right) % pixels, 0)
            inside = (
                (row >= down) & (row < side + down) & (col >= right) & (col < side + right)
            )
            moved = jnp.where(inside, moved, 0.0)
        shifted[:, tap * cols : (tap + 1) * cols] = moved.astype(bf16)

    demod_grad = jnp.zeros((8, cols), f32)
    for start in range(0, channels, block):
        for tap in range(0, KTAPS, 2):
            taps = min(2, KTAPS - tap)
            result = jnp.dot(
                scaled_t[start : start + block],
                shifted[:, tap * cols : (tap + taps) * cols],
                preferred_element_type=f32,
            )
            for own in range(taps):
                first = (tap + own) * channels + start
                part = result[:, own * cols : (own + 1) * cols]
                product[first : first + block] = part
                weighted = part * weight_ref[first : first + block].astype(f32)
                demod_grad = demod_grad + jnp.sum(weighted.reshape(-1, 8, cols), axis=0)
    demod_grad = jnp.sum(demod_grad, axis=0, keepdims=True) / demodulate
    square_grad = -0.5 * demodulate * demodulate * demodulate * demod_grad

    demod_part = lax.dot_general(
        jnp.broadcast_to(square_grad, (8, cols)),
        square[...],
        (((1,), (1,)), ((), ())),
        precision=highest,
        preferred_element_type=f32,
    )[:1]
    style_rows = []
    for start in range(0, channels, block):
        kernel = jnp.concatenate(
            [
                weight_ref[tap * channels + start : tap * channels + start + block]
                for tap in range(KTAPS)
            ],
            axis=1,
        )
        inner = lax.dot_general(
            shifted[...], kernel, (((1,), (1,)), ((), ())), preferred_element_type=f32
        )
        total = jnp.sum(inner * feat_ref[:, start : start + block].astype(f32), axis=0, keepdims=True)
        total = total + 2.0 * style[:, start : start + block] * demod_part[:, start : start + block]
        for own in range(block // cols):
            inner_ref[start // cols + own] = inner[:, own * cols : (own + 1) * cols]
            style_rows.append(total[:, own * cols : (own + 1) * cols])
    tile = jnp.concatenate(
        style_rows + [jnp.broadcast_to(source_ref[...], (8, cols))], axis=0
    )
    for peer in range(tile_ref.shape[0]):
        tile_ref[peer] = tile

    for start in range(0, channels, LANES):
        columns = jnp.broadcast_to(style_sq[:1, start : start + LANES], (LANES, LANES)).T
        factor[start : start + LANES] = columns * (2.0 * square_grad)

    per_row = sent_ref.shape[1] // rows_dev
    for row in range(sent_ref.shape[0]):
        for target in (sent_ref, kept_ref):
            target[row, per_row * rows_dev :] = jnp.zeros((8, cols), f32)

    ncore = 2
    departures = [
        pltpu.make_async_copy(sent_ref.at[row], sent_hbm.at[row], out_sems.at[row])
        for row in range(sent_ref.shape[0])
    ]

    def emit(even_ref, odd_ref):
        total = KTAPS * channels
        first = 0
        while first < total:
            chunk, at = divmod(first, rows_dev)
            source = first % channels
            size = min(rows_dev - at, channels - source)
            target = odd_ref if chunk % 2 else even_ref
            row, place = divmod(chunk // 2, per_row)
            at += place * rows_dev
            target[row, at : at + size] = product[first : first + size] + weight_ref[
                first : first + size
            ].astype(f32) * factor[source : source + size]
            first += size
            if first % (ncore * per_row * rows_dev) == 0:
                departures[row].start()
        for departure in departures:
            departure.wait()

    @pl.when(core_ref[0] == 0)
    def _():
        emit(kept_ref, sent_ref)

    @pl.when(core_ref[0] != 0)
    def _():
        emit(sent_ref, kept_ref)


def convolution_part(core_id, features, styles, weight, grad_out, source, sizes):
    far, near, rows_dev, peers = sizes
    pixels, channels = features.shape
    cols = grad_out.shape[1]
    side = int(round(pixels**0.5))
    f32 = jnp.float32
    whole = pl.BlockSpec(memory_space=pltpu.VMEM)
    away = pl.BlockSpec(memory_space=pltpu.HBM)
    tile_rows = channels // LANES + 8
    return pl.pallas_call(
        functools.partial(convolution_kernel, side, rows_dev),
        out_shape=(
            pltpu.HBM((far, near * rows_dev + 8, cols), f32),
            jax.ShapeDtypeStruct((far, near * rows_dev + 8, cols), f32),
            jax.ShapeDtypeStruct((channels // cols, pixels, cols), f32),
            jax.ShapeDtypeStruct((peers, tile_rows, cols), f32),
        ),
        in_specs=[pl.BlockSpec(memory_space=pltpu.SMEM)] + [away] * 4 + [whole],
        out_specs=[away] + [whole] * 3,
        scratch_shapes=[
            pltpu.VMEM((pixels, channels), jnp.bfloat16),
            pltpu.VMEM((1, channels), f32),
            pltpu.VMEM((KTAPS * channels, cols), jnp.bfloat16),
            pltpu.VMEM((pixels, cols), jnp.bfloat16),
            pltpu.VMEM((far, near * rows_dev + 8, cols), f32),
            pltpu.VMEM((channels, pixels), jnp.bfloat16),
            pltpu.VMEM((pixels, KTAPS * cols), jnp.bfloat16),
            pltpu.VMEM((KTAPS * channels, cols), f32),
            pltpu.VMEM((channels, cols), f32),
            pltpu.VMEM((channels, cols), f32),
            pltpu.SemaphoreType.DMA((4,)),
            pltpu.SemaphoreType.DMA((far,)),
        ],
        compiler_params=pltpu.CompilerParams(vmem_limit_bytes=32 * 1024 * 1024),
        cost_estimate=pl.CostEstimate(
            flops=4 * pixels * KTAPS * channels * cols, transcendentals=0, bytes_accessed=12_000_000
        ),
        name="convolution_part",
    )(
        core_id.astype(jnp.int32).reshape(1),
        *(
            pltpu.with_memory_space_constraint(one, pltpu.HBM)
            for one in (features, styles, weight, grad_out)
        ),
        source,
    )


def gathered_from(rows, name, hops):
    size = lax.axis_size(name)
    return jnp.concatenate(
        [rows]
        + [
            lax.ppermute(rows, name, [(sender, (sender + hop) % size) for sender in range(size)])
            for hop in hops
        ],
        axis=0,
    )


def halved(blocks, bit):
    side = (lax.axis_index("chan") // bit) % 2
    pairs = blocks.reshape((-1, 2) + blocks.shape[1:])
    coming = lax.ppermute(
        lax.dynamic_index_in_dim(pairs, 1 - side, 1, keepdims=False),
        "chan",
        [(sender, sender ^ bit) for sender in range(lax.axis_size("chan"))],
    )
    return lax.dynamic_index_in_dim(pairs, side, 1, keepdims=False) + coming


def exchange(blocks, axes):
    return lax.all_to_all(blocks, axes, 0, 0, tiled=True)


def local(
    features, styles, conv_weight, grad_out, crossover, partner, latents, map_pre, map_weight
):
    samples, side_len, _, channels = features.shape
    cols_dev = conv_weight.shape[2]
    pixels = samples * side_len * side_len
    nx, nz, ncore, nchan = (lax.axis_size(name) for name in ("x", "z", "core", "chan"))
    batch_size = nx * nz * ncore
    rows_dev = KTAPS * channels // batch_size
    chan_id = lax.axis_index("chan")
    dp_id = (lax.axis_index("x") * nz + lax.axis_index("z")) * ncore + lax.axis_index("core")

    own_rows = jnp.concatenate(
        [latents.reshape(1, -1, LANES), map_pre.reshape(1, -1, LANES)], axis=1
    )
    pair = gathered_from(own_rows, "core", (1,))
    map_rows = exchange(map_weight.reshape(nchan, -1, cols_dev), "chan")

    core_id = lax.axis_index("core")
    source = jnp.where(crossover <= LAYER, partner, dp_id).astype(jnp.float32)
    sent, kept, inner_part, tile = convolution_part(
        core_id,
        features.reshape(pixels, channels),
        styles,
        conv_weight.reshape(KTAPS * channels, cols_dev),
        grad_out.reshape(pixels, cols_dev),
        jnp.broadcast_to(source[:, None], (1, cols_dev)),
        (nx, nz, rows_dev, ncore * nchan),
    )
    tile, sent, map_rows, pair = lax.optimization_barrier((tile, sent, map_rows, pair))
    parts = exchange(tile, ("core", "chan")).reshape(ncore, nchan, -1, LANES)
    coming = lax.ppermute(sent, "core", [(core, ncore - 1 - core) for core in range(ncore)])
    inner_half = halved(inner_part, 1)
    style_grad = jnp.sum(parts[:, :, :-8], axis=1)
    hidden_rows = jnp.sum(
        lax.dot_general(
            map_rows,
            style_grad.reshape(ncore, nchan, cols_dev),
            (((2,), (2,)), ((0,), (1,))),
            precision=highest,
        ),
        axis=0,
    ).T
    style_rows = lax.dynamic_slice_in_dim(
        style_grad.reshape(ncore, nchan, cols_dev), chan_id, 1, 1
    ).reshape(ncore, cols_dev)
    riders = jnp.concatenate(
        [style_rows, hidden_rows, parts[:, 0, -1], jnp.zeros((8 - 3 * ncore, cols_dev))], axis=0
    )
    near = gathered_from(pair, "z", range(1, min(4, nz)))
    coming, riders, near = lax.optimization_barrier((coming, riders, near))
    moved = exchange(
        kept
        + coming
        + jnp.pad(
            jnp.broadcast_to(riders[None], (nx,) + riders.shape),
            ((0, 0), (nz * rows_dev, 0), (0, 0)),
        ),
        "x",
    )
    gathered = gathered_from(near, "z", range(4, nz, 4))
    pieces = jnp.sum(moved[:, : nz * rows_dev], axis=0).reshape(nz, rows_dev, cols_dev)
    riders = jnp.concatenate(
        [
            moved[:, nz * rows_dev + kind * ncore : nz * rows_dev + (kind + 1) * ncore].reshape(
                nx * ncore, cols_dev
            )
            for kind in range(3)
        ],
        axis=0,
    )
    pieces, riders, gathered, inner_half = lax.optimization_barrier(
        (pieces, riders, gathered, inner_half)
    )
    moved = exchange(
        jnp.concatenate([pieces, jnp.broadcast_to(riders[None], (nz,) + riders.shape)], axis=1), "z"
    )
    gathered = gathered_from(gathered, "x", range(1, nx))
    back_x, back_z, back_core = np.meshgrid(
        np.arange(nx), np.arange(nz), np.arange(ncore), indexing="ij"
    )
    spots = [
        (lax.axis_index(name) + lax.axis_size(name) - back.reshape(-1)) % lax.axis_size(name)
        for name, back in (("x", back_x), ("z", back_z), ("core", back_core))
    ]
    row_ids = ((spots[0] * nz + spots[1]) * ncore + spots[2]).astype(jnp.float32)
    group = inner_half.shape[0]
    place = chan_id // 2
    grad_inner = lax.dynamic_index_in_dim(inner_half, place, 0, keepdims=False)
    for flip in range(1, group):
        grad_inner = grad_inner + lax.ppermute(
            lax.dynamic_index_in_dim(inner_half, place ^ flip, 0, keepdims=False),
            "chan",
            [(sender, sender ^ (2 * flip)) for sender in range(nchan)],
        )
    style_cols = lax.dynamic_slice_in_dim(styles, chan_id * cols_dev, cols_dev, 1)
    grad_input = (grad_inner * style_cols).astype(jnp.bfloat16)
    grad_weight = jnp.sum(moved[:, :rows_dev], axis=0) / batch_size

    per = nx * ncore
    style_all, hidden_all, source_all = (
        moved[:, rows_dev + kind * per : rows_dev + (kind + 1) * per].reshape(batch_size, cols_dev)
        for kind in range(3)
    )
    matches = (
        source_all[:, :1] == row_ids[None, :]
    ).astype(jnp.float32)
    received = lax.dot_general(
        matches,
        jnp.concatenate([style_all, hidden_all], axis=1),
        (((0,), (0,)), ((), ())),
        precision=highest,
    )
    incoming, hidden_grad = received[:, :cols_dev], received[:, cols_dev:]
    half = channels // LANES
    all_latents = gathered[:, :half].reshape(batch_size, -1)
    all_pre = gathered[:, half:].reshape(batch_size, -1)
    hidden = jnp.where(all_pre > 0, all_pre, 0.2 * all_pre)
    grad_map_out = (
        lax.dot_general(hidden, incoming, (((0,), (0,)), ((), ())), precision=lax.Precision.HIGH) / batch_size
    )
    pre_cols = lax.dynamic_slice_in_dim(all_pre, chan_id * cols_dev, cols_dev, 1)
    pre_grad = hidden_grad * jnp.where(pre_cols > 0, 1.0, 0.2)
    grad_map_in = (
        lax.dot_general(all_latents, pre_grad, (((0,), (0,)), ((), ())), precision=lax.Precision.HIGH)
        / batch_size
    )
    return (
        grad_weight,
        grad_input.reshape(samples, side_len, side_len, cols_dev),
        grad_map_out,
        grad_map_in,
    )


def solution(mesh):
    dp_count, chan_count = mesh.devices.shape
    split = Mesh(
        mesh.devices.reshape(dp_axes(dp_count) + (chan_count,)), ("x", "z", "core", "chan")
    )
    dp = ("x", "z", "core")
    in_specs = (
        P(dp, None, None, None),
        P(dp, None),
        P(None, None, "chan"),
        P(dp, None, None, "chan"),
        P(dp),
        P(dp),
        P(dp, None),
        P(dp, None),
        P(None, "chan"),
    )
    out_specs = (P(dp, "chan"), P(dp, None, None, "chan"), P(None, "chan"), P(None, "chan"))
    return jax.shard_map(local, mesh=split, in_specs=in_specs, out_specs=out_specs, check_vma=False)
```

```python
import functools

import jax
import jax.numpy as jnp
import numpy as np
from jax import lax
from jax.experimental import pallas as pl
from jax.experimental.pallas import tpu as pltpu
from jax.sharding import Mesh, PartitionSpec as P

KTAPS = 9
LAYER = 6
LANES = 128

highest = lax.Precision.HIGHEST


def dp_axes(dp_count):
    return (4, 12, 2) if dp_count == 96 else (2, dp_count // 4, 2)


def convolution_kernel(
    side, rows_dev, core_ref, feat_hbm, style_hbm, weight_hbm, grad_hbm, source_ref,
    sent_hbm, kept_ref, inner_ref, tile_ref,
    feat_ref, style_ref, weight_ref, grad_ref, sent_ref,
    scaled_t, shifted, product, square, factor, in_sems, out_sems,
):
    pixels, channels = feat_ref.shape
    cols = grad_ref.shape[1]
    block = min(256, channels)
    f32, bf16 = jnp.float32, jnp.bfloat16

    arrivals = [
        pltpu.make_async_copy(source, target, in_sems.at[at])
        for at, (source, target) in enumerate(
            (
                (style_hbm, style_ref),
                (feat_hbm, feat_ref),
                (weight_hbm, weight_ref),
                (grad_hbm, grad_ref),
            )
        )
    ]
    for arrival in arrivals:
        arrival.start()
    arrivals[0].wait()
    arrivals[1].wait()
    style = style_ref[...]
    for start in range(0, channels, block):
        wide = feat_ref[:, start : start + block].astype(f32) * style[:, start : start + block]
        scaled_t[start : start + block] = wide.astype(bf16).astype(f32).T.astype(bf16)
    arrivals[2].wait()
    arrivals[3].wait()

    for start in range(0, channels, LANES):
        total = jnp.zeros((LANES, cols), f32)
        for tap in range(KTAPS):
            wide = weight_ref[tap * channels + start : tap * channels + start + LANES].astype(f32)
            total = total + wide * wide
        square[start : start + LANES] = total
    style_sq = jnp.broadcast_to(style * style, (8, channels))
    norm = jnp.dot(style_sq, square[...], precision=highest, preferred_element_type=f32)
    demodulate = lax.rsqrt(norm[:1] + 1e-08)

    grad_scaled = (grad_ref[...].astype(f32) * demodulate).astype(bf16).astype(f32)
    place = lax.broadcasted_iota(jnp.int32, (pixels, cols), 0)
    row, col = place // side, place % side
    for tap in range(KTAPS):
        down, right = tap // 3 - 1, tap % 3 - 1
        moved = grad_scaled
        if down or right:
            moved = pltpu.roll(grad_scaled, (down * side + right) % pixels, 0)
            inside = (
                (row >= down) & (row < side + down) & (col >= right) & (col < side + right)
            )
            moved = jnp.where(inside, moved, 0.0)
        shifted[:, tap * cols : (tap + 1) * cols] = moved.astype(bf16)

    demod_grad = jnp.zeros((8, cols), f32)
    for start in range(0, channels, block):
        for tap in range(0, KTAPS, 2):
            taps = min(2, KTAPS - tap)
            result = jnp.dot(
                scaled_t[start : start + block],
                shifted[:, tap * cols : (tap + taps) * cols],
                preferred_element_type=f32,
            )
            for own in range(taps):
                first = (tap + own) * channels + start
                part = result[:, own * cols : (own + 1) * cols]
                product[first : first + block] = part
                weighted = part * weight_ref[first : first + block].astype(f32)
                demod_grad = demod_grad + jnp.sum(weighted.reshape(-1, 8, cols), axis=0)
    demod_grad = jnp.sum(demod_grad, axis=0, keepdims=True) / demodulate
    square_grad = -0.5 * demodulate * demodulate * demodulate * demod_grad

    demod_part = lax.dot_general(
        jnp.broadcast_to(square_grad, (8, cols)),
        square[...],
        (((1,), (1,)), ((), ())),
        precision=highest,
        preferred_element_type=f32,
    )[:1]
    style_rows = []
    for start in range(0, channels, block):
        kernel = jnp.concatenate(
            [
                weight_ref[tap * channels + start : tap * channels + start + block]
                for tap in range(KTAPS)
            ],
            axis=1,
        )
        inner = lax.dot_general(
            shifted[...], kernel, (((1,), (1,)), ((), ())), preferred_element_type=f32
        )
        total = jnp.sum(inner * feat_ref[:, start : start + block].astype(f32), axis=0, keepdims=True)
        total = total + 2.0 * style[:, start : start + block] * demod_part[:, start : start + block]
        for own in range(block // cols):
            inner_ref[start // cols + own] = inner[:, own * cols : (own + 1) * cols]
            style_rows.append(total[:, own * cols : (own + 1) * cols])
    tile = jnp.concatenate(
        style_rows + [jnp.broadcast_to(source_ref[...], (8, cols))], axis=0
    )
    for peer in range(tile_ref.shape[0]):
        tile_ref[peer] = tile

    for start in range(0, channels, LANES):
        columns = jnp.broadcast_to(style_sq[:1, start : start + LANES], (LANES, LANES)).T
        factor[start : start + LANES] = columns * (2.0 * square_grad)

    per_row = sent_ref.shape[1] // rows_dev
    for row in range(sent_ref.shape[0]):
        for target in (sent_ref, kept_ref):
            target[row, per_row * rows_dev :] = jnp.zeros((8, cols), f32)

    ncore = 2
    departures = [
        pltpu.make_async_copy(sent_ref.at[row], sent_hbm.at[row], out_sems.at[row])
        for row in range(sent_ref.shape[0])
    ]

    def emit(even_ref, odd_ref):
        total = KTAPS * channels
        first = 0
        while first < total:
            chunk, at = divmod(first, rows_dev)
            source = first % channels
            size = min(rows_dev - at, channels - source)
            target = odd_ref if chunk % 2 else even_ref
            row, place = divmod(chunk // 2, per_row)
            at += place * rows_dev
            target[row, at : at + size] = product[first : first + size] + weight_ref[
                first : first + size
            ].astype(f32) * factor[source : source + size]
            first += size
            if first % (ncore * per_row * rows_dev) == 0:
                departures[row].start()
        for departure in departures:
            departure.wait()

    @pl.when(core_ref[0] == 0)
    def _():
        emit(kept_ref, sent_ref)

    @pl.when(core_ref[0] != 0)
    def _():
        emit(sent_ref, kept_ref)


def convolution_part(core_id, features, styles, weight, grad_out, source, sizes):
    far, near, rows_dev, peers = sizes
    pixels, channels = features.shape
    cols = grad_out.shape[1]
    side = int(round(pixels**0.5))
    f32 = jnp.float32
    whole = pl.BlockSpec(memory_space=pltpu.VMEM)
    away = pl.BlockSpec(memory_space=pltpu.HBM)
    tile_rows = channels // LANES + 8
    return pl.pallas_call(
        functools.partial(convolution_kernel, side, rows_dev),
        out_shape=(
            pltpu.HBM((far, near * rows_dev + 8, cols), f32),
            jax.ShapeDtypeStruct((far, near * rows_dev + 8, cols), f32),
            jax.ShapeDtypeStruct((channels // cols, pixels, cols), f32),
            jax.ShapeDtypeStruct((peers, tile_rows, cols), f32),
        ),
        in_specs=[pl.BlockSpec(memory_space=pltpu.SMEM)] + [away] * 4 + [whole],
        out_specs=[away] + [whole] * 3,
        scratch_shapes=[
            pltpu.VMEM((pixels, channels), jnp.bfloat16),
            pltpu.VMEM((1, channels), f32),
            pltpu.VMEM((KTAPS * channels, cols), jnp.bfloat16),
            pltpu.VMEM((pixels, cols), jnp.bfloat16),
            pltpu.VMEM((far, near * rows_dev + 8, cols), f32),
            pltpu.VMEM((channels, pixels), jnp.bfloat16),
            pltpu.VMEM((pixels, KTAPS * cols), jnp.bfloat16),
            pltpu.VMEM((KTAPS * channels, cols), f32),
            pltpu.VMEM((channels, cols), f32),
            pltpu.VMEM((channels, cols), f32),
            pltpu.SemaphoreType.DMA((4,)),
            pltpu.SemaphoreType.DMA((far,)),
        ],
        compiler_params=pltpu.CompilerParams(vmem_limit_bytes=32 * 1024 * 1024),
        cost_estimate=pl.CostEstimate(
            flops=4 * pixels * KTAPS * channels * cols, transcendentals=0, bytes_accessed=12_000_000
        ),
        name="convolution_part",
    )(
        core_id.astype(jnp.int32).reshape(1),
        *(
            pltpu.with_memory_space_constraint(one, pltpu.HBM)
            for one in (features, styles, weight, grad_out)
        ),
        source,
    )


def arriving(rows, name, hops):
    size = lax.axis_size(name)
    return [
        lax.ppermute(rows, name, [(sender, (sender + hop) % size) for sender in range(size)])
        for hop in hops
    ]


def halved(blocks, bit):
    side = (lax.axis_index("chan") // bit) % 2
    pairs = blocks.reshape((-1, 2) + blocks.shape[1:])
    coming = lax.ppermute(
        lax.dynamic_index_in_dim(pairs, 1 - side, 1, keepdims=False),
        "chan",
        [(sender, sender ^ bit) for sender in range(lax.axis_size("chan"))],
    )
    return lax.dynamic_index_in_dim(pairs, side, 1, keepdims=False) + coming


def exchange(blocks, axes):
    return lax.all_to_all(blocks, axes, 0, 0, tiled=True)


def local(
    features, styles, conv_weight, grad_out, crossover, partner, latents, map_pre, map_weight
):
    samples, side_len, _, channels = features.shape
    cols_dev = conv_weight.shape[2]
    pixels = samples * side_len * side_len
    nx, nz, ncore, nchan = (lax.axis_size(name) for name in ("x", "z", "core", "chan"))
    batch_size = nx * nz * ncore
    rows_dev = KTAPS * channels // batch_size
    chan_id = lax.axis_index("chan")
    dp_id = (lax.axis_index("x") * nz + lax.axis_index("z")) * ncore + lax.axis_index("core")

    own_rows = jnp.concatenate(
        [latents.reshape(1, -1, LANES), map_pre.reshape(1, -1, LANES)], axis=1
    )
    map_rows = exchange(map_weight.reshape(nchan, -1, cols_dev), "chan")

    core_id = lax.axis_index("core")
    source = jnp.where(crossover <= LAYER, partner, dp_id).astype(jnp.float32)
    sent, kept, inner_part, tile = convolution_part(
        core_id,
        features.reshape(pixels, channels),
        styles,
        conv_weight.reshape(KTAPS * channels, cols_dev),
        grad_out.reshape(pixels, cols_dev),
        jnp.broadcast_to(source[:, None], (1, cols_dev)),
        (nx, nz, rows_dev, ncore * nchan),
    )
    tile, sent, map_rows, own_rows = lax.optimization_barrier((tile, sent, map_rows, own_rows))
    parts = exchange(tile, ("core", "chan")).reshape(ncore, nchan, -1, LANES)
    coming = lax.ppermute(sent, "core", [(core, ncore - 1 - core) for core in range(ncore)])
    inner_half = halved(inner_part, 1)
    style_grad = jnp.sum(parts[:, :, :-8], axis=1)
    hidden_rows = jnp.sum(
        lax.dot_general(
            map_rows,
            style_grad.reshape(ncore, nchan, cols_dev),
            (((2,), (2,)), ((0,), (1,))),
            precision=highest,
        ),
        axis=0,
    ).T
    style_rows = lax.dynamic_slice_in_dim(
        style_grad.reshape(ncore, nchan, cols_dev), chan_id, 1, 1
    ).reshape(ncore, cols_dev)
    riders = jnp.concatenate(
        [style_rows, hidden_rows, parts[:, 0, -1], jnp.zeros((8 - 3 * ncore, cols_dev))], axis=0
    )
    near = arriving(own_rows, "z", range(1, min(4, nz)))
    coming, riders, near = lax.optimization_barrier((coming, riders, near))
    moved = exchange(
        kept
        + coming
        + jnp.pad(
            jnp.broadcast_to(riders[None], (nx,) + riders.shape),
            ((0, 0), (nz * rows_dev, 0), (0, 0)),
        ),
        "x",
    )
    near = jnp.concatenate([own_rows] + near, axis=0)
    gathered = jnp.concatenate([near] + arriving(near, "z", range(4, nz, 4)), axis=0)
    gathered = jnp.concatenate([gathered] + arriving(gathered, "core", (1,)), axis=0)
    pieces = jnp.sum(moved[:, : nz * rows_dev], axis=0).reshape(nz, rows_dev, cols_dev)
    riders = jnp.concatenate(
        [
            moved[:, nz * rows_dev + kind * ncore : nz * rows_dev + (kind + 1) * ncore].reshape(
                nx * ncore, cols_dev
            )
            for kind in range(3)
        ],
        axis=0,
    )
    pieces, riders, gathered, inner_half = lax.optimization_barrier(
        (pieces, riders, gathered, inner_half)
    )
    moved = exchange(
        jnp.concatenate([pieces, jnp.broadcast_to(riders[None], (nz,) + riders.shape)], axis=1), "z"
    )
    gathered = jnp.concatenate([gathered] + arriving(gathered, "x", range(1, nx)), axis=0)
    back_x, back_core, back_z = np.meshgrid(
        np.arange(nx), np.arange(ncore), np.arange(nz), indexing="ij"
    )
    spots = [
        (lax.axis_index(name) + lax.axis_size(name) - back.reshape(-1)) % lax.axis_size(name)
        for name, back in (("x", back_x), ("z", back_z), ("core", back_core))
    ]
    row_ids = ((spots[0] * nz + spots[1]) * ncore + spots[2]).astype(jnp.float32)
    group = inner_half.shape[0]
    place = chan_id // 2
    grad_inner = lax.dynamic_index_in_dim(inner_half, place, 0, keepdims=False)
    for flip in range(1, group):
        grad_inner = grad_inner + lax.ppermute(
            lax.dynamic_index_in_dim(inner_half, place ^ flip, 0, keepdims=False),
            "chan",
            [(sender, sender ^ (2 * flip)) for sender in range(nchan)],
        )
    style_cols = lax.dynamic_slice_in_dim(styles, chan_id * cols_dev, cols_dev, 1)
    grad_input = (grad_inner * style_cols).astype(jnp.bfloat16)
    grad_weight = jnp.sum(moved[:, :rows_dev], axis=0) / batch_size

    per = nx * ncore
    style_all, hidden_all, source_all = (
        moved[:, rows_dev + kind * per : rows_dev + (kind + 1) * per].reshape(batch_size, cols_dev)
        for kind in range(3)
    )
    matches = (
        source_all[:, :1] == row_ids[None, :]
    ).astype(jnp.float32)
    received = lax.dot_general(
        matches,
        jnp.concatenate([style_all, hidden_all], axis=1),
        (((0,), (0,)), ((), ())),
        precision=highest,
    )
    incoming, hidden_grad = received[:, :cols_dev], received[:, cols_dev:]
    half = channels // LANES
    all_latents = gathered[:, :half].reshape(batch_size, -1)
    all_pre = gathered[:, half:].reshape(batch_size, -1)
    hidden = jnp.where(all_pre > 0, all_pre, 0.2 * all_pre)
    grad_map_out = (
        lax.dot_general(hidden, incoming, (((0,), (0,)), ((), ())), precision=lax.Precision.HIGH) / batch_size
    )
    pre_cols = lax.dynamic_slice_in_dim(all_pre, chan_id * cols_dev, cols_dev, 1)
    pre_grad = hidden_grad * jnp.where(pre_cols > 0, 1.0, 0.2)
    grad_map_in = (
        lax.dot_general(all_latents, pre_grad, (((0,), (0,)), ((), ())), precision=lax.Precision.HIGH)
        / batch_size
    )
    return (
        grad_weight,
        grad_input.reshape(samples, side_len, side_len, cols_dev),
        grad_map_out,
        grad_map_in,
    )


def solution(mesh):
    dp_count, chan_count = mesh.devices.shape
    split = Mesh(
        mesh.devices.reshape(dp_axes(dp_count) + (chan_count,)), ("x", "z", "core", "chan")
    )
    dp = ("x", "z", "core")
    in_specs = (
        P(dp, None, None, None),
        P(dp, None),
        P(None, None, "chan"),
        P(dp, None, None, "chan"),
        P(dp),
        P(dp),
        P(dp, None),
        P(dp, None),
        P(None, "chan"),
    )
    out_specs = (P(dp, "chan"), P(dp, None, None, "chan"), P(None, "chan"), P(None, "chan"))
    return jax.shard_map(local, mesh=split, in_specs=in_specs, out_specs=out_specs, check_vma=False)
```

```python
import functools

import jax
import jax.numpy as jnp
import numpy as np
from jax import lax
from jax.experimental import pallas as pl
from jax.experimental.pallas import tpu as pltpu
from jax.sharding import Mesh, PartitionSpec as P

KTAPS = 9
LAYER = 6
LANES = 128

highest = lax.Precision.HIGHEST


def dp_axes(dp_count):
    return (4, 12, 2) if dp_count == 96 else (2, dp_count // 4, 2)


def convolution_kernel(
    side, rows_dev, core_ref, feat_hbm, style_hbm, weight_hbm, grad_hbm, source_ref,
    sent_hbm, kept_ref, inner_ref, tile_ref,
    feat_ref, style_ref, weight_ref, grad_ref, sent_ref,
    scaled_t, shifted, product, square, factor, in_sems, out_sems,
):
    pixels, channels = feat_ref.shape
    cols = grad_ref.shape[1]
    block = min(256, channels)
    f32, bf16 = jnp.float32, jnp.bfloat16

    arrivals = [
        pltpu.make_async_copy(source, target, in_sems.at[at])
        for at, (source, target) in enumerate(
            (
                (style_hbm, style_ref),
                (feat_hbm, feat_ref),
                (weight_hbm, weight_ref),
                (grad_hbm, grad_ref),
            )
        )
    ]
    for arrival in arrivals:
        arrival.start()
    arrivals[0].wait()
    arrivals[1].wait()
    style = style_ref[...]
    for start in range(0, channels, block):
        wide = feat_ref[:, start : start + block].astype(f32) * style[:, start : start + block]
        scaled_t[start : start + block] = wide.astype(bf16).astype(f32).T.astype(bf16)
    arrivals[2].wait()
    arrivals[3].wait()

    for start in range(0, channels, LANES):
        total = jnp.zeros((LANES, cols), f32)
        for tap in range(KTAPS):
            wide = weight_ref[tap * channels + start : tap * channels + start + LANES].astype(f32)
            total = total + wide * wide
        square[start : start + LANES] = total
    style_sq = jnp.broadcast_to(style * style, (8, channels))
    norm = jnp.dot(style_sq, square[...], precision=highest, preferred_element_type=f32)
    demodulate = lax.rsqrt(norm[:1] + 1e-08)

    grad_scaled = (grad_ref[...].astype(f32) * demodulate).astype(bf16).astype(f32)
    place = lax.broadcasted_iota(jnp.int32, (pixels, cols), 0)
    row, col = place // side, place % side
    for tap in range(KTAPS):
        down, right = tap // 3 - 1, tap % 3 - 1
        moved = grad_scaled
        if down or right:
            moved = pltpu.roll(grad_scaled, (down * side + right) % pixels, 0)
            inside = (
                (row >= down) & (row < side + down) & (col >= right) & (col < side + right)
            )
            moved = jnp.where(inside, moved, 0.0)
        shifted[:, tap * cols : (tap + 1) * cols] = moved.astype(bf16)

    demod_grad = jnp.zeros((8, cols), f32)
    for start in range(0, channels, block):
        for tap in range(0, KTAPS, 2):
            taps = min(2, KTAPS - tap)
            result = jnp.dot(
                scaled_t[start : start + block],
                shifted[:, tap * cols : (tap + taps) * cols],
                preferred_element_type=f32,
            )
            for own in range(taps):
                first = (tap + own) * channels + start
                part = result[:, own * cols : (own + 1) * cols]
                product[first : first + block] = part
                weighted = part * weight_ref[first : first + block].astype(f32)
                demod_grad = demod_grad + jnp.sum(weighted.reshape(-1, 8, cols), axis=0)
    demod_grad = jnp.sum(demod_grad, axis=0, keepdims=True) / demodulate
    square_grad = -0.5 * demodulate * demodulate * demodulate * demod_grad

    demod_part = lax.dot_general(
        jnp.broadcast_to(square_grad, (8, cols)),
        square[...],
        (((1,), (1,)), ((), ())),
        precision=highest,
        preferred_element_type=f32,
    )[:1]
    style_rows = []
    for start in range(0, channels, block):
        kernel = jnp.concatenate(
            [
                weight_ref[tap * channels + start : tap * channels + start + block]
                for tap in range(KTAPS)
            ],
            axis=1,
        )
        inner = lax.dot_general(
            shifted[...], kernel, (((1,), (1,)), ((), ())), preferred_element_type=f32
        )
        total = jnp.sum(inner * feat_ref[:, start : start + block].astype(f32), axis=0, keepdims=True)
        total = total + 2.0 * style[:, start : start + block] * demod_part[:, start : start + block]
        for own in range(block // cols):
            inner_ref[start // cols + own] = inner[:, own * cols : (own + 1) * cols]
            style_rows.append(total[:, own * cols : (own + 1) * cols])
    tile = jnp.concatenate(
        style_rows + [jnp.broadcast_to(source_ref[...], (8, cols))], axis=0
    )
    for peer in range(tile_ref.shape[0]):
        tile_ref[peer] = tile

    for start in range(0, channels, LANES):
        columns = jnp.broadcast_to(style_sq[:1, start : start + LANES], (LANES, LANES)).T
        factor[start : start + LANES] = columns * (2.0 * square_grad)

    per_row = sent_ref.shape[1] // rows_dev
    for row in range(sent_ref.shape[0]):
        for target in (sent_ref, kept_ref):
            target[row, per_row * rows_dev :] = jnp.zeros((8, cols), f32)

    ncore = 2
    departures = [
        pltpu.make_async_copy(sent_ref.at[row], sent_hbm.at[row], out_sems.at[row])
        for row in range(sent_ref.shape[0])
    ]

    def emit(even_ref, odd_ref):
        total = KTAPS * channels
        first = 0
        while first < total:
            chunk, at = divmod(first, rows_dev)
            source = first % channels
            size = min(rows_dev - at, channels - source)
            target = odd_ref if chunk % 2 else even_ref
            row, place = divmod(chunk // 2, per_row)
            at += place * rows_dev
            target[row, at : at + size] = product[first : first + size] + weight_ref[
                first : first + size
            ].astype(f32) * factor[source : source + size]
            first += size
            if first % (ncore * per_row * rows_dev) == 0:
                departures[row].start()
        for departure in departures:
            departure.wait()

    @pl.when(core_ref[0] == 0)
    def _():
        emit(kept_ref, sent_ref)

    @pl.when(core_ref[0] != 0)
    def _():
        emit(sent_ref, kept_ref)


def convolution_part(core_id, features, styles, weight, grad_out, source, sizes):
    far, near, rows_dev, peers = sizes
    pixels, channels = features.shape
    cols = grad_out.shape[1]
    side = int(round(pixels**0.5))
    f32 = jnp.float32
    whole = pl.BlockSpec(memory_space=pltpu.VMEM)
    away = pl.BlockSpec(memory_space=pltpu.HBM)
    tile_rows = channels // LANES + 8
    return pl.pallas_call(
        functools.partial(convolution_kernel, side, rows_dev),
        out_shape=(
            pltpu.HBM((far, near * rows_dev + 8, cols), f32),
            jax.ShapeDtypeStruct((far, near * rows_dev + 8, cols), f32),
            jax.ShapeDtypeStruct((channels // cols, pixels, cols), f32),
            jax.ShapeDtypeStruct((peers, tile_rows, cols), f32),
        ),
        in_specs=[pl.BlockSpec(memory_space=pltpu.SMEM)] + [away] * 4 + [whole],
        out_specs=[away] + [whole] * 3,
        scratch_shapes=[
            pltpu.VMEM((pixels, channels), jnp.bfloat16),
            pltpu.VMEM((1, channels), f32),
            pltpu.VMEM((KTAPS * channels, cols), jnp.bfloat16),
            pltpu.VMEM((pixels, cols), jnp.bfloat16),
            pltpu.VMEM((far, near * rows_dev + 8, cols), f32),
            pltpu.VMEM((channels, pixels), jnp.bfloat16),
            pltpu.VMEM((pixels, KTAPS * cols), jnp.bfloat16),
            pltpu.VMEM((KTAPS * channels, cols), f32),
            pltpu.VMEM((channels, cols), f32),
            pltpu.VMEM((channels, cols), f32),
            pltpu.SemaphoreType.DMA((4,)),
            pltpu.SemaphoreType.DMA((far,)),
        ],
        compiler_params=pltpu.CompilerParams(vmem_limit_bytes=32 * 1024 * 1024),
        cost_estimate=pl.CostEstimate(
            flops=4 * pixels * KTAPS * channels * cols, transcendentals=0, bytes_accessed=12_000_000
        ),
        name="convolution_part",
    )(
        core_id.astype(jnp.int32).reshape(1),
        *(
            pltpu.with_memory_space_constraint(one, pltpu.HBM)
            for one in (features, styles, weight, grad_out)
        ),
        source,
    )


def arriving(rows, name, hops):
    size = lax.axis_size(name)
    return [
        lax.ppermute(rows, name, [(sender, (sender + hop) % size) for sender in range(size)])
        for hop in hops
    ]


def halved(blocks, bit):
    side = (lax.axis_index("chan") // bit) % 2
    pairs = blocks.reshape((-1, 2) + blocks.shape[1:])
    coming = lax.ppermute(
        lax.dynamic_index_in_dim(pairs, 1 - side, 1, keepdims=False),
        "chan",
        [(sender, sender ^ bit) for sender in range(lax.axis_size("chan"))],
    )
    return lax.dynamic_index_in_dim(pairs, side, 1, keepdims=False) + coming


def exchange(blocks, axes):
    return lax.all_to_all(blocks, axes, 0, 0, tiled=True)


def local(
    features, styles, conv_weight, grad_out, crossover, partner, latents, map_pre, map_weight
):
    samples, side_len, _, channels = features.shape
    cols_dev = conv_weight.shape[2]
    pixels = samples * side_len * side_len
    nx, nz, ncore, nchan = (lax.axis_size(name) for name in ("x", "z", "core", "chan"))
    batch_size = nx * nz * ncore
    rows_dev = KTAPS * channels // batch_size
    chan_id = lax.axis_index("chan")
    dp_id = (lax.axis_index("x") * nz + lax.axis_index("z")) * ncore + lax.axis_index("core")

    own_rows = jnp.concatenate(
        [latents.reshape(1, -1, LANES), map_pre.reshape(1, -1, LANES)], axis=1
    )
    pair = jnp.concatenate([own_rows] + arriving(own_rows, "core", (1,)), axis=0)
    map_rows = exchange(map_weight.reshape(nchan, -1, cols_dev), "chan")

    core_id = lax.axis_index("core")
    source = jnp.where(crossover <= LAYER, partner, dp_id).astype(jnp.float32)
    sent, kept, inner_part, tile = convolution_part(
        core_id,
        features.reshape(pixels, channels),
        styles,
        conv_weight.reshape(KTAPS * channels, cols_dev),
        grad_out.reshape(pixels, cols_dev),
        jnp.broadcast_to(source[:, None], (1, cols_dev)),
        (nx, nz, rows_dev, ncore * nchan),
    )
    tile, sent, map_rows, pair = lax.optimization_barrier((tile, sent, map_rows, pair))
    parts = exchange(tile, ("core", "chan")).reshape(ncore, nchan, -1, LANES)
    coming = lax.ppermute(sent, "core", [(core, ncore - 1 - core) for core in range(ncore)])
    inner_half = halved(inner_part, 1)
    style_grad = jnp.sum(parts[:, :, :-8], axis=1)
    hidden_rows = jnp.sum(
        lax.dot_general(
            map_rows,
            style_grad.reshape(ncore, nchan, cols_dev),
            (((2,), (2,)), ((0,), (1,))),
            precision=highest,
        ),
        axis=0,
    ).T
    style_rows = lax.dynamic_slice_in_dim(
        style_grad.reshape(ncore, nchan, cols_dev), chan_id, 1, 1
    ).reshape(ncore, cols_dev)
    riders = jnp.concatenate(
        [style_rows, hidden_rows, parts[:, 0, -1], jnp.zeros((8 - 3 * ncore, cols_dev))], axis=0
    )
    near = arriving(pair, "z", range(1, min(4, nz)))
    coming, riders, near = lax.optimization_barrier((coming, riders, near))
    moved = exchange(
        kept
        + coming
        + jnp.pad(
            jnp.broadcast_to(riders[None], (nx,) + riders.shape),
            ((0, 0), (nz * rows_dev, 0), (0, 0)),
        ),
        "x",
    )
    near = lax.optimization_barrier(jnp.concatenate([pair] + near, axis=0))
    gathered = jnp.concatenate([near] + arriving(near, "z", range(4, nz, 4)), axis=0)
    pieces = jnp.sum(moved[:, : nz * rows_dev], axis=0).reshape(nz, rows_dev, cols_dev)
    riders = jnp.concatenate(
        [
            moved[:, nz * rows_dev + kind * ncore : nz * rows_dev + (kind + 1) * ncore].reshape(
                nx * ncore, cols_dev
            )
            for kind in range(3)
        ],
        axis=0,
    )
    pieces, riders, gathered, inner_half = lax.optimization_barrier(
        (pieces, riders, gathered, inner_half)
    )
    moved = exchange(
        jnp.concatenate([pieces, jnp.broadcast_to(riders[None], (nz,) + riders.shape)], axis=1), "z"
    )
    gathered = jnp.concatenate([gathered] + arriving(gathered, "x", range(1, nx)), axis=0)
    back_x, back_z, back_core = np.meshgrid(
        np.arange(nx), np.arange(nz), np.arange(ncore), indexing="ij"
    )
    spots = [
        (lax.axis_index(name) + lax.axis_size(name) - back.reshape(-1)) % lax.axis_size(name)
        for name, back in (("x", back_x), ("z", back_z), ("core", back_core))
    ]
    row_ids = ((spots[0] * nz + spots[1]) * ncore + spots[2]).astype(jnp.float32)
    group = inner_half.shape[0]
    place = chan_id // 2
    grad_inner = lax.dynamic_index_in_dim(inner_half, place, 0, keepdims=False)
    for flip in range(1, group):
        grad_inner = grad_inner + lax.ppermute(
            lax.dynamic_index_in_dim(inner_half, place ^ flip, 0, keepdims=False),
            "chan",
            [(sender, sender ^ (2 * flip)) for sender in range(nchan)],
        )
    style_cols = lax.dynamic_slice_in_dim(styles, chan_id * cols_dev, cols_dev, 1)
    grad_input = (grad_inner * style_cols).astype(jnp.bfloat16)
    grad_weight = jnp.sum(moved[:, :rows_dev], axis=0) / batch_size

    per = nx * ncore
    style_all, hidden_all, source_all = (
        moved[:, rows_dev + kind * per : rows_dev + (kind + 1) * per].reshape(batch_size, cols_dev)
        for kind in range(3)
    )
    matches = (
        source_all[:, :1] == row_ids[None, :]
    ).astype(jnp.float32)
    received = lax.dot_general(
        matches,
        jnp.concatenate([style_all, hidden_all], axis=1),
        (((0,), (0,)), ((), ())),
        precision=highest,
    )
    incoming, hidden_grad = received[:, :cols_dev], received[:, cols_dev:]
    half = channels // LANES
    all_latents = gathered[:, :half].reshape(batch_size, -1)
    all_pre = gathered[:, half:].reshape(batch_size, -1)
    hidden = jnp.where(all_pre > 0, all_pre, 0.2 * all_pre)
    grad_map_out = (
        lax.dot_general(hidden, incoming, (((0,), (0,)), ((), ())), precision=lax.Precision.HIGH) / batch_size
    )
    pre_cols = lax.dynamic_slice_in_dim(all_pre, chan_id * cols_dev, cols_dev, 1)
    pre_grad = hidden_grad * jnp.where(pre_cols > 0, 1.0, 0.2)
    grad_map_in = (
        lax.dot_general(all_latents, pre_grad, (((0,), (0,)), ((), ())), precision=lax.Precision.HIGH)
        / batch_size
    )
    return (
        grad_weight,
        grad_input.reshape(samples, side_len, side_len, cols_dev),
        grad_map_out,
        grad_map_in,
    )


def solution(mesh):
    dp_count, chan_count = mesh.devices.shape
    split = Mesh(
        mesh.devices.reshape(dp_axes(dp_count) + (chan_count,)), ("x", "z", "core", "chan")
    )
    dp = ("x", "z", "core")
    in_specs = (
        P(dp, None, None, None),
        P(dp, None),
        P(None, None, "chan"),
        P(dp, None, None, "chan"),
        P(dp),
        P(dp),
        P(dp, None),
        P(dp, None),
        P(None, "chan"),
    )
    out_specs = (P(dp, "chan"), P(dp, None, None, "chan"), P(None, "chan"), P(None, "chan"))
    return jax.shard_map(local, mesh=split, in_specs=in_specs, out_specs=out_specs, check_vma=False)
```
